128 devices in a mesh: branch: 16 (over z, y_hi, core), scen: 8 (over x, y_lo).
Axes of the slice: x: 4, y: 4 (y_hi: 2, y_lo: 2; y = y_hi * 2 + y_lo), z: 4, core: 2. Of those that a mesh axis runs over, the one named last changes fastest.
Arguments:
- counts: int32 [128], P(('branch', 'scen')), may hold values from 1 to 4, as said below
- blocks: int32 [512], P(('branch', 'scen')), may hold values from 0 to 31, as said below
- factors: float32 [512, 512, 512], P(('branch', 'scen')), as said below
- b_first: float32 [512, 512, 512], P(('branch', 'scen')), may hold values from -0.2 to 0.2
- b_branch: float32 [512, 512, 512], P(('branch', 'scen')), may hold values from -0.8 to 0.8
- c_first: float32 [512, 512], replicated, may hold values from -6 to 6
- c_band: float32 [16384, 512], P(('branch', 'scen')), may hold values from -4 to 4
- c_diag: float32 [32, 512, 512], P('branch', 'scen'), may hold values from -6 to 6
Outputs:
- schur_first: float32 [512, 512], replicated
- schur_band: float32 [16384, 512], P(('branch', 'scen'))
- schur_diag: float32 [32, 512, 512], P('branch', 'scen')
The draws below stay inside these ranges and needn't reach their ends.
Inputs may be any that keep to these rules, and one draw needn't show every extreme that they name: `counts`: every device holds one or more scenarios; some device holds 4. `blocks`: A slot of a device on branch index b names a block between 2 * b and 2 * b + 1. `factors`: each factor is lower triangular with a diagonal between 1 and 3 and off-diagonal entries of order 512 ** -0.5.
All inputs are finite; a program needn't handle non-finite values.
Results may differ from the reference program's by a relative error of at most 0.0003.
Values sent between devices are 32-bit elements; how exact they have to be, the bound alone decides.
A program may use at most 128 MiB of HBM per device.

```python
import jax
import jax.numpy as jnp
from jax import lax

NS = 512
W = 512
CAP = 4
BLK_BR = 2
NBLK = 32
SLOTS = 512
N_BRANCH = 16
N_SCEN = 8


def draw_counts(key, part):
    key_heavy, key_light, key_small = jax.random.split(key, 3)
    device_total = N_BRANCH * N_SCEN
    branch_of = jnp.arange(device_total) // N_SCEN
    branch_ids = jnp.arange(N_BRANCH)
    forced_heavy = (branch_ids == 0) | (branch_ids == N_BRANCH - 1)
    forced_light = (branch_ids == N_BRANCH // 2) | (branch_ids == N_BRANCH // 2 - 1)
    heavy_draw = jax.random.randint(key_heavy, (N_BRANCH,), 0, 8) == 0
    heavy_branch = forced_heavy | heavy_draw & jnp.logical_not(forced_light)
    light_count = 1 + jax.random.randint(key_light, (device_total,), 0, 3)
    small_count = 1 + jax.random.randint(key_small, (device_total,), 0, 2)
    light_pick = jnp.where(forced_light[branch_of], small_count, light_count)
    return jnp.where(heavy_branch[branch_of], CAP, light_pick).astype(jnp.int32)


def draw_blocks(key, part):
    slot_total = CAP * N_BRANCH * N_SCEN
    branch_of = jnp.arange(slot_total) // (CAP * N_SCEN)
    offset = jax.random.randint(key, (slot_total,), 0, BLK_BR)
    return (BLK_BR * branch_of + offset).astype(jnp.int32)


def draw_factors(key, part):
    key_diag, key_off = jax.random.split(key, 2)
    slot_total = CAP * N_BRANCH * N_SCEN
    diag_vals = jax.random.uniform(key_diag, (slot_total, NS), jnp.float32, 1.0, 2.0)
    off_scale = 0.5
    lower_part = jax.random.normal(key_off, (slot_total, NS, NS), jnp.float32) * (off_scale / NS ** 0.5)
    lower_part = jnp.tril(lower_part, -1)
    identity = jnp.eye(NS, dtype=jnp.float32)
    return lower_part + diag_vals[:, :, None] * identity[None, :, :]


def steps_of(rng, shape, cuts, low, high):
    loudness = 1.0
    for position, parts in cuts:
        draws = jax.random.uniform(jax.random.fold_in(jax.random.fold_in(rng, 6), position), (parts,), jnp.float32, low / len(cuts), high / len(cuts))
        loudness = loudness * jnp.repeat(jnp.exp(draws), shape[position] // parts).reshape((-1,) + (1,) * (len(shape) - 1 - position))
    return loudness


def gaussian(rng, extent, scale, reach, cuts=(), kind=jnp.bfloat16):
    entries = scale * jax.random.normal(rng, extent, jnp.float32)
    if cuts:
        entries = entries * steps_of(rng, extent, cuts, -0.22, 0.18)
    return jnp.clip(entries, -reach, reach).astype(kind)


def setup_inputs(seed: int = 0) -> dict:
    streams_of = jax.random.split(jax.random.key(seed), 9)
    return {
        "counts": draw_counts(jax.random.fold_in(streams_of[8], 71), 0),
        "blocks": draw_blocks(jax.random.fold_in(streams_of[8], 71), 0),
        "factors": draw_factors(jax.random.fold_in(streams_of[8], 71), 0),
        "b_first": gaussian(streams_of[3], (SLOTS, NS, W), 0.0316, 0.2, ((0, 128),), jnp.float32),
        "b_branch": gaussian(streams_of[4], (SLOTS, NS, W), 0.126, 0.8, ((0, 128),), jnp.float32),
        "c_first": gaussian(streams_of[5], (W, W), 1.0, 6.0, (), jnp.float32),
        "c_band": gaussian(streams_of[6], (NBLK * W, W), 0.5, 4.0, ((0, 128),), jnp.float32),
        "c_diag": gaussian(streams_of[7], (NBLK, W, W), 1.0, 6.0, ((0, 16), (1, 8)), jnp.float32),
    }


def scenario_terms(factor, first_cols, second_cols):
    block_width = first_cols.shape[1]
    rhs = jnp.concatenate([first_cols, second_cols], axis=1)
    solved = jax.scipy.linalg.solve_triangular(factor, rhs, lower=True)
    first_y = solved[:, :block_width]
    second_y = solved[:, block_width:]
    dims = (((0,), (0,)), ((), ()))
    first_term = lax.dot_general(first_y.astype(jnp.float32), first_y.astype(jnp.float32), dims, precision=lax.Precision.HIGHEST, preferred_element_type=jnp.float32)
    row_term = lax.dot_general(second_y.astype(jnp.float32), solved.astype(jnp.float32), dims, precision=lax.Precision.HIGHEST, preferred_element_type=jnp.float32)
    return (first_term, row_term)

def reference(counts, blocks, factors, b_first, b_branch, c_first, c_band, c_diag):
    block_width = c_first.shape[0]
    block_total = c_diag.shape[0]
    slot_total = factors.shape[0]
    first_sum = jnp.zeros((block_width, block_width), jnp.float32)
    band_sum = jnp.zeros((block_total, block_width, block_width), jnp.float32)
    diag_sum = jnp.zeros((block_total, block_width, block_width), jnp.float32)

    def add_slot(state_now, inputs):
        factor, first_cols, second_cols, block_id, slot_index = inputs
        is_live = slot_index % CAP < counts[slot_index // CAP]

        def add_terms(state_in):
            first_acc, band_acc, diag_acc = state_in
            first_term, row_term = scenario_terms(factor, first_cols, second_cols)
            band_now = lax.dynamic_index_in_dim(band_acc, block_id, 0, keepdims=False)
            diag_now = lax.dynamic_index_in_dim(diag_acc, block_id, 0, keepdims=False)
            band_acc = lax.dynamic_update_index_in_dim(band_acc, band_now + row_term[:, :block_width], block_id, 0)
            diag_acc = lax.dynamic_update_index_in_dim(diag_acc, diag_now + row_term[:, block_width:], block_id, 0)
            return (first_acc + first_term, band_acc, diag_acc)
        return (lax.cond(is_live, add_terms, lambda state_in: state_in, state_now), None)
    slot_ids = jnp.arange(slot_total, dtype=jnp.int32)
    result, _ = lax.scan(add_slot, (first_sum, band_sum, diag_sum), (factors, b_first, b_branch, blocks.astype(jnp.int32), slot_ids))
    first_sum, band_sum, diag_sum = result
    schur_first = c_first - first_sum
    schur_band = c_band - band_sum.reshape(block_total * block_width, block_width)
    schur_diag = c_diag - diag_sum
    return (schur_first, schur_band, schur_diag)
```

```python
import jax
import jax.numpy as jnp
from jax import lax
from jax.experimental import pallas as pl
from jax.experimental.pallas import tpu as pltpu
from jax.sharding import PartitionSpec as P

F32, BF16 = jnp.float32, jnp.bfloat16


def split(value):
    high = value.astype(BF16)
    return high, (value - high.astype(F32)).astype(BF16)


def dot3(left, right, dims):
    (lh, ll), (rh, rl) = left, right
    one = lambda a, b: lax.dot_general(a, b, (dims, ((), ())), preferred_element_type=F32)
    return one(lh, rl) + one(ll, rh) + one(lh, rh)


NN = ((1,), (0,))
TN = ((0,), (0,))


def on_diagonal(wide):
    lane = lax.broadcasted_iota(jnp.int32, wide.shape, 1)
    left = lane < wide.shape[0]
    zero = jnp.zeros_like(wide)
    return jnp.concatenate([jnp.where(left, wide, zero), jnp.where(left, zero, wide)], axis=0)


def pair_inverses(wides):
    rows, cols = wides[0].shape
    r = lax.broadcasted_iota(jnp.int32, (rows, cols), 0)
    c = lax.broadcasted_iota(jnp.int32, (rows, cols), 1) & (rows - 1)
    eye = r == c
    out = []
    for wide in wides:
        pivots = jnp.where(eye, wide, 0.0)
        by_col = 1.0 / jnp.sum(pivots, axis=0, keepdims=True)
        by_row = 1.0 / jnp.concatenate(
            [
                jnp.broadcast_to(jnp.sum(pivots[:, i : i + rows], axis=1, keepdims=True), (rows, rows))
                for i in range(0, cols, rows)
            ],
            axis=1,
        )
        pairs = ((r >> 1) == (c >> 1)) & (r > c)
        out.append(jnp.where(eye, by_row, 0.0) - jnp.where(pairs, wide * by_col * by_row, 0.0))
    shift = 1
    while (1 << shift) < rows:
        below = ((r >> (shift + 1)) == (c >> (shift + 1))) & ((r >> shift) > (c >> shift))
        inv = [split(x) for x in out]
        inv_on = [split(on_diagonal(x)) for x in out]
        mid = [dot3(split(jnp.where(below, w, 0.0)), x, NN) for w, x in zip(wides, inv_on)]
        mid_on = [split(on_diagonal(m)) for m in mid]
        out = [x - dot3(xs, m, NN) for x, xs, m in zip(out, inv, mid_on)]
        shift += 1
    return out


def half_inverses(factor, half):
    q = half // 2
    wides = []
    for start in (0, half):
        a = factor[start : start + q, start : start + q]
        d = factor[start + q : start + half, start + q : start + half]
        wides.append(jnp.concatenate([a, d], axis=1))
    invs = pair_inverses(wides)
    full = []
    for start, wide in zip((0, half), invs):
        a, d = split(wide[:, :q]), split(wide[:, q:])
        low = split(factor[start + q : start + half, start : start + q])
        corner = -dot3(d, split(dot3(low, a, NN)), NN)
        top = jnp.concatenate([wide[:, :q], jnp.zeros((q, q), F32)], axis=1)
        full.append(jnp.concatenate([top, jnp.concatenate([corner, wide[:, q:]], axis=1)], axis=0))
    return full


def compute_kernel(counts, blocks, fac_hbm, bf_hbm, bb_hbm, first, band, diag, fac, rhs, yh, yl, sems):
    n, w = fac_hbm.shape[1], bf_hbm.shape[2]
    half = n // 2
    live = counts[0]

    def loads(s):
        return (
            pltpu.make_async_copy(fac_hbm.at[s], fac.at[s], sems.at[s, 0]),
            pltpu.make_async_copy(bf_hbm.at[s], rhs.at[s, :, pl.ds(0, w)], sems.at[s, 1]),
            pltpu.make_async_copy(bb_hbm.at[s], rhs.at[s, :, pl.ds(w, w)], sems.at[s, 2]),
        )

    @pl.loop(0, live)
    def _(s):
        for copy in loads(s):
            copy.start()

    first[...] = jnp.zeros_like(first)
    band[...] = jnp.zeros_like(band)
    diag[...] = jnp.zeros_like(diag)

    @pl.loop(0, live)
    def _(s):
        load_f, load_a, load_b = loads(s)
        load_f.wait()
        factor = fac.at[s]
        inv_top, inv_low = (split(x) for x in half_inverses(factor, half))
        link = split(factor[half:, :half])
        load_a.wait()
        load_b.wait()
        for col in range(0, 2 * w, half):
            cols = pl.ds(col, half)
            top = dot3(inv_top, split(rhs[s, :half, cols]), NN)
            top_s = split(top)
            yh[:half, cols], yl[:half, cols] = top_s
            low = dot3(inv_low, split(rhs[s, half:, cols] - dot3(link, top_s, NN)), NN)
            yh[half:, cols], yl[half:, cols] = split(low)
        k = blocks[s] & 1
        for i in range(0, 2 * w, half):
            left = (yh[:, pl.ds(i, half)], yl[:, pl.ds(i, half)])
            for j in range(0, i + half, half):
                if i >= w and j >= w and j > i:
                    continue
                right = (yh[:, pl.ds(j, half)], yl[:, pl.ds(j, half)])
                term = dot3(left, right, TN)
                if i < w:
                    first[pl.ds(i, half), pl.ds(j, half)] += term
                elif j < w:
                    band[k, pl.ds(i - w, half), pl.ds(j, half)] += term
                else:
                    diag[k, pl.ds(i - w, half), pl.ds(j - w, half)] += term

    first[:half, half:] = first[half:, :half].T
    for k in range(diag.shape[0]):
        diag[k, :half, half:] = diag[k, half:, :half].T


def local_sums(counts, blocks, factors, b_first, b_branch, block_count):
    cap, n, w = b_first.shape
    smem = pl.BlockSpec(memory_space=pltpu.SMEM)
    hbm = pl.BlockSpec(memory_space=pl.ANY)
    vmem = pl.BlockSpec(memory_space=pltpu.VMEM)
    return pl.pallas_call(
        compute_kernel,
        out_shape=(
            jax.ShapeDtypeStruct((w, w), F32),
            jax.ShapeDtypeStruct((block_count, w, w), F32),
            jax.ShapeDtypeStruct((block_count, w, w), F32),
        ),
        in_specs=[smem, smem, hbm, hbm, hbm],
        out_specs=(vmem, vmem, vmem),
        scratch_shapes=[
            pltpu.VMEM((cap, n, n), F32),
            pltpu.VMEM((cap, n, 2 * w), F32),
            pltpu.VMEM((n, 2 * w), BF16),
            pltpu.VMEM((n, 2 * w), BF16),
            pltpu.SemaphoreType.DMA((cap, 3)),
        ],
        compiler_params=pltpu.CompilerParams(vmem_limit_bytes=48 << 20),
        name="local_sums",
    )(counts, blocks, factors, b_first, b_branch)


def shards(counts, blocks, factors, b_first, b_branch, c_first, c_band, c_diag):
    first, band, diag = local_sums(counts, blocks, factors, b_first, b_branch, c_diag.shape[0])
    band = band.reshape(-1, band.shape[-1])
    band_sum = lax.psum_scatter(band, "scen", scatter_dimension=0, tiled=True)
    diag_sum = lax.psum_scatter(diag, "scen", scatter_dimension=1, tiled=True)
    first_sum = lax.psum(first, ("branch", "scen"))
    return (c_first - first_sum, c_band - band_sum, c_diag - diag_sum)


def solution(mesh):
    placed = (
        P(("branch", "scen")),
        P(("branch", "scen")),
        P(("branch", "scen"), None, None),
        P(("branch", "scen"), None, None),
        P(("branch", "scen"), None, None),
        P(),
        P(("branch", "scen"), None),
        P("branch", "scen", None),
    )
    return jax.shard_map(
        shards,
        mesh=mesh,
        in_specs=placed,
        out_specs=(P(), P(("branch", "scen"), None), P("branch", "scen", None)),
        check_vma=False,
    )
```

```python
import jax
import jax.numpy as jnp
from jax import lax
from jax.experimental import pallas as pl
from jax.experimental.pallas import tpu as pltpu
from jax.sharding import PartitionSpec as P

F32, BF16 = jnp.float32, jnp.bfloat16


def split(value):
    high = value.astype(BF16)
    return high, (value - high.astype(F32)).astype(BF16)


def dot3(left, right, dims):
    (lh, ll), (rh, rl) = left, right
    one = lambda a, b: lax.dot_general(a, b, (dims, ((), ())), preferred_element_type=F32)
    return one(lh, rl) + one(ll, rh) + one(lh, rh)


NN = ((1,), (0,))
TN = ((0,), (0,))


def on_diagonal(wide):
    lane = lax.broadcasted_iota(jnp.int32, wide.shape, 1)
    left = lane < wide.shape[0]
    zero = jnp.zeros_like(wide)
    return jnp.concatenate([jnp.where(left, wide, zero), jnp.where(left, zero, wide)], axis=0)


def pair_inverses(wides):
    rows, cols = wides[0].shape
    r = lax.broadcasted_iota(jnp.int32, (rows, cols), 0)
    c = lax.broadcasted_iota(jnp.int32, (rows, cols), 1) & (rows - 1)
    eye = r == c
    out = []
    for wide in wides:
        pivots = jnp.where(eye, wide, 0.0)
        by_col = 1.0 / jnp.sum(pivots, axis=0, keepdims=True)
        by_row = 1.0 / jnp.concatenate(
            [
                jnp.broadcast_to(jnp.sum(pivots[:, i : i + rows], axis=1, keepdims=True), (rows, rows))
                for i in range(0, cols, rows)
            ],
            axis=1,
        )
        pairs = ((r >> 1) == (c >> 1)) & (r > c)
        out.append(jnp.where(eye, by_row, 0.0) - jnp.where(pairs, wide * by_col * by_row, 0.0))
    shift = 1
    while (1 << shift) < rows:
        below = ((r >> (shift + 1)) == (c >> (shift + 1))) & ((r >> shift) > (c >> shift))
        inv = [split(x) for x in out]
        inv_on = [split(on_diagonal(x)) for x in out]
        mid = [dot3(split(jnp.where(below, w, 0.0)), x, NN) for w, x in zip(wides, inv_on)]
        mid_on = [split(on_diagonal(m)) for m in mid]
        out = [x - dot3(xs, m, NN) for x, xs, m in zip(out, inv, mid_on)]
        shift += 1
    return out


def half_inverses(factor, half):
    q = half // 2
    wides = []
    for start in (0, half):
        a = factor[start : start + q, start : start + q]
        d = factor[start + q : start + half, start + q : start + half]
        wides.append(jnp.concatenate([a, d], axis=1))
    invs = pair_inverses(wides)
    full = []
    for start, wide in zip((0, half), invs):
        a, d = split(wide[:, :q]), split(wide[:, q:])
        low = split(factor[start + q : start + half, start : start + q])
        corner = -dot3(d, split(dot3(low, a, NN)), NN)
        top = jnp.concatenate([wide[:, :q], jnp.zeros((q, q), F32)], axis=1)
        full.append(jnp.concatenate([top, jnp.concatenate([corner, wide[:, q:]], axis=1)], axis=0))
    return full


def compute_kernel(counts, blocks, fac_hbm, bf_hbm, bb_hbm, first, band, diag, fac, rhs, yh, yl, sems):
    n, w = fac_hbm.shape[1], bf_hbm.shape[2]
    half = n // 2
    live = counts[0]

    def loads(s):
        return (
            pltpu.make_async_copy(fac_hbm.at[s], fac.at[s], sems.at[s, 0]),
            pltpu.make_async_copy(bf_hbm.at[s], rhs.at[s, :, pl.ds(0, w)], sems.at[s, 1]),
            pltpu.make_async_copy(bb_hbm.at[s], rhs.at[s, :, pl.ds(w, w)], sems.at[s, 2]),
        )

    @pl.loop(0, live)
    def _(s):
        for copy in loads(s):
            copy.start()

    first[...] = jnp.zeros_like(first)
    band[...] = jnp.zeros_like(band)
    diag[...] = jnp.zeros_like(diag)

    @pl.loop(0, live)
    def _(s):
        load_f, load_a, load_b = loads(s)
        load_f.wait()
        factor = fac.at[s]
        inv_top, inv_low = (split(x) for x in half_inverses(factor, half))
        link = split(factor[half:, :half])
        load_a.wait()
        load_b.wait()
        for col in range(0, 2 * w, half):
            cols = pl.ds(col, half)
            top = dot3(inv_top, split(rhs[s, :half, cols]), NN)
            top_s = split(top)
            yh[:half, cols], yl[:half, cols] = top_s
            low = dot3(inv_low, split(rhs[s, half:, cols] - dot3(link, top_s, NN)), NN)
            yh[half:, cols], yl[half:, cols] = split(low)
        k = blocks[s] & 1
        for i in range(0, 2 * w, half):
            left = (yh[:, pl.ds(i, half)], yl[:, pl.ds(i, half)])
            for j in range(0, i + half, half):
                if i >= w and j >= w and j > i:
                    continue
                right = (yh[:, pl.ds(j, half)], yl[:, pl.ds(j, half)])
                term = dot3(left, right, TN)
                if i < w:
                    first[pl.ds(i, half), pl.ds(j, half)] += term
                elif j < w:
                    band[k, pl.ds(i - w, half), pl.ds(j, half)] += term
                else:
                    diag[k, pl.ds(i - w, half), pl.ds(j - w, half)] += term

    first[:half, half:] = first[half:, :half].T
    for k in range(diag.shape[0]):
        diag[k, :half, half:] = diag[k, half:, :half].T


def local_sums(counts, blocks, factors, b_first, b_branch, block_count):
    cap, n, w = b_first.shape
    smem = pl.BlockSpec(memory_space=pltpu.SMEM)
    hbm = pl.BlockSpec(memory_space=pl.ANY)
    vmem = pl.BlockSpec(memory_space=pltpu.VMEM)
    return pl.pallas_call(
        compute_kernel,
        out_shape=(
            jax.ShapeDtypeStruct((w, w), F32),
            jax.ShapeDtypeStruct((block_count, w, w), F32),
            jax.ShapeDtypeStruct((block_count, w, w), F32),
        ),
        in_specs=[smem, smem, hbm, hbm, hbm],
        out_specs=(vmem, vmem, vmem),
        scratch_shapes=[
            pltpu.VMEM((cap, n, n), F32),
            pltpu.VMEM((cap, n, 2 * w), F32),
            pltpu.VMEM((n, 2 * w), BF16),
            pltpu.VMEM((n, 2 * w), BF16),
            pltpu.SemaphoreType.DMA((cap, 3)),
        ],
        compiler_params=pltpu.CompilerParams(vmem_limit_bytes=48 << 20),
        name="local_sums",
    )(counts, blocks, factors, b_first, b_branch)


class Net:
    def __init__(self, send_sems, recv_sems):
        self.sems = (send_sems, recv_sems)
        self.count = 0
        self.sent = []

    def send(self, source, target, device):
        copy = pltpu.make_async_remote_copy(
            src_ref=source,
            dst_ref=target,
            send_sem=self.sems[0].at[self.count],
            recv_sem=self.sems[1].at[self.count],
            device_id=device,
            device_id_type=pl.DeviceIdType.MESH,
        )
        copy.start()
        self.count += 1
        self.sent.append(copy)
        return copy

    def drain(self):
        for copy in self.sent:
            copy.wait_send()


FAR, NEXT, PREV, OWN = 0, 1, 2, 3
OFFSETS = (2, 1, 3, 0)


class Ring:
    def __init__(self, net, piece, up, down, far_in, out, near_in):
        self.net, self.piece, self.up, self.down = net, piece, up, down
        self.far_in, self.out, self.near_in = far_in, out, near_in

    def far(self):
        self.far_up = self.net.send(self.piece(FAR, 0), self.far_in.at[0], self.up)
        self.far_down = self.net.send(self.piece(FAR, 1), self.far_in.at[1], self.down)

    def near_up(self):
        self.n01 = self.net.send(self.piece(NEXT, 1), self.near_in.at[0, 1], self.up)

    def near_down(self):
        self.n10 = self.net.send(self.piece(PREV, 0), self.near_in.at[1, 0], self.down)

    def mid_up(self):
        self.far_up.wait_recv()
        self.out[0] = self.piece(NEXT, 0)[...] + self.far_in[0]
        self.n00 = self.net.send(self.out.at[0], self.near_in.at[0, 0], self.up)

    def mid_down(self):
        self.far_down.wait_recv()
        self.out[1] = self.piece(PREV, 1)[...] + self.far_in[1]
        self.n11 = self.net.send(self.out.at[1], self.near_in.at[1, 1], self.down)

    def end(self):
        for copy in (self.n01, self.n10, self.n00, self.n11):
            copy.wait_recv()
        return [self.piece(OWN, h)[...] + self.near_in[0, h] + self.near_in[1, h] for h in range(2)]


def exchange_kernel(
    first, band, diag, cf_hbm, cb_hbm, cd_hbm, out_f, out_b, out_d,
    cf, cb, cd, core_in, held, z_far, z_out, z_near, z_sum, y_in, x_all, full,
    b_far, b_out, b_near, b_send, b_in, b_keep, d_in, d_far, d_out, d_near, send_sems, recv_sems, c_sems,
):
    b, s = lax.axis_index("branch"), lax.axis_index("scen")
    z, y_hi, core = b // 4, (b // 2) % 2, b % 2
    x, y_lo = s // 2, s % 2
    y = 2 * y_hi + y_lo
    w = first.shape[1]
    half = w // 2
    halves = (pl.ds(0, half), pl.ds(half, half))
    net = Net(send_sems, recv_sems)

    other_core = (b + 1 - 2 * core, s)
    z_up, z_down = (((z + 1) % 4) * 4 + b % 4, s), (((z + 3) % 4) * 4 + b % 4, s)
    y_peers = []
    for d in (1, 2, 3):
        there = (y + d) % 4
        y_peers.append((z * 4 + (there // 2) * 2 + core, x * 2 + there % 2))
    x_peers = [(b, ((x + d) % 4) * 2 + y_lo) for d in (1, 2, 3)]
    x_up, x_down = x_peers[0], x_peers[2]
    y_near = (b, x * 2 + 1 - y_lo)

    c_copies = [
        pltpu.make_async_copy(source, target, c_sems.at[i])
        for i, (source, target) in enumerate(((cf_hbm, cf), (cb_hbm, cb), (cd_hbm, cd)))
    ]
    for copy in c_copies:
        copy.start()

    barrier = pltpu.get_barrier_semaphore()
    greeted = [other_core, z_up, z_down] + y_peers + x_peers
    for peer in greeted:
        pl.semaphore_signal(barrier, inc=1, device_id=peer, device_id_type=pl.DeviceIdType.MESH)
    pl.semaphore_wait(barrier, len(greeted))

    rows_core = pl.multiple_of(core * half, half)
    core_rows, core_far = pl.ds(rows_core, half), pl.ds(pl.multiple_of((1 - core) * half, half), half)
    core_copy = net.send(first.at[core_far], core_in, other_core)

    sub = band.shape[0] // 8
    bands = []
    for chunk, y_to in enumerate((1 - y_lo, y_lo)):

        def band_piece(role, h, y_to=y_to):
            start = ((x + OFFSETS[role]) % 4) * (2 * sub) + y_to * sub
            return band.at[pl.ds(pl.multiple_of(start, sub), sub), halves[h]]

        bands.append(Ring(net, band_piece, x_up, x_down, b_far.at[chunk], b_out.at[chunk], b_near.at[chunk]))
    drow = diag.shape[1] // 8

    def diag_rows(role, y_to):
        start = ((x + OFFSETS[role]) % 4) * (2 * drow) + y_to * drow
        return diag.at[:, pl.ds(pl.multiple_of(start, drow), drow), :]

    def diag_send(role):
        return net.send(diag_rows(role, 1 - y_lo), d_in.at[role], y_near)

    def diag_take(copy, role):
        copy.wait_recv()
        d_in[role] += diag_rows(role, y_lo)[...]

    diags = Ring(net, lambda role, h: d_in.at[role, :, :, halves[h]], x_up, x_down, d_far, d_out, d_near)

    zrow = half // 4
    z_ring = Ring(
        net,
        lambda role, h: held.at[pl.ds(pl.multiple_of(((z + OFFSETS[role]) % 4) * zrow, zrow), zrow), halves[h]],
        z_up, z_down, z_far, z_out, z_near,
    )

    bands[0].far()
    d0 = diag_send(FAR)
    bands[1].far()
    bands[0].near_up()
    bands[0].near_down()

    core_copy.wait_recv()
    held[...] = first[core_rows] + core_in[...]
    z_ring.far()
    z_ring.near_up()
    z_ring.near_down()
    d1 = diag_send(NEXT)
    bands[0].mid_up()
    bands[0].mid_down()
    z_ring.mid_up()
    z_ring.mid_down()
    diag_take(d0, FAR)
    diags.far()

    z_sum[:, :half], z_sum[:, half:] = z_ring.end()
    yrow = zrow // 4
    y_copies = []
    for d in (1, 2, 3):
        piece = z_sum.at[pl.ds(pl.multiple_of(((y + d) % 4) * yrow, yrow), yrow)]
        y_copies.append(net.send(piece, y_in.at[d - 1], y_peers[d - 1]))
    d2 = diag_send(PREV)
    bands[1].mid_up()
    bands[1].mid_down()
    for copy in y_copies:
        copy.wait_recv()
    own = z_sum[pl.ds(pl.multiple_of(y * yrow, yrow), yrow)]
    x_all[x] = own + y_in[0] + y_in[1] + y_in[2]
    x_copies = [net.send(x_all.at[x], x_all.at[x], peer) for peer in x_peers]
    bands[1].near_up()
    bands[1].near_down()
    diag_take(d1, NEXT)
    diags.near_up()
    diags.mid_up()

    for copy in x_copies:
        copy.wait_recv()
    z_rows = rows_core + z * zrow
    y_rows = pl.ds(pl.multiple_of(z_rows + y * yrow, yrow), yrow)
    full[y_rows] = (x_all[0] + x_all[1]) + (x_all[2] + x_all[3])
    y_back = [net.send(full.at[y_rows], full.at[y_rows], peer) for peer in y_peers]
    d3 = diag_send(OWN)
    b_send[:, :half], b_send[:, half:] = bands[0].end()
    cross = net.send(b_send, b_in, y_near)
    diag_take(d2, PREV)
    diags.near_down()
    diags.mid_down()

    for copy in y_back:
        copy.wait_recv()

    def z_block(offset):
        return pl.ds(pl.multiple_of(rows_core + ((z + offset) % 4) * zrow, zrow), zrow)

    mine = full.at[z_block(0)]
    up_copy, down_copy = net.send(mine, mine, z_up), net.send(mine, mine, z_down)
    core_backs = [net.send(mine, mine, other_core)]
    b_keep[:, :half], b_keep[:, half:] = bands[1].end()
    up_copy.wait_recv()
    below = full.at[z_block(3)]
    pass_up = net.send(full.at[z_block(3), halves[0]], full.at[z_block(3), halves[0]], z_up)
    core_backs.append(net.send(below, below, other_core))
    down_copy.wait_recv()
    above = full.at[z_block(1)]
    pass_down = net.send(full.at[z_block(1), halves[1]], full.at[z_block(1), halves[1]], z_down)
    core_backs.append(net.send(above, above, other_core))
    for copy in c_copies:
        copy.wait()
    diag_take(d3, OWN)
    pass_up.wait_recv()
    pass_down.wait_recv()
    far = full.at[z_block(2)]
    core_backs.append(net.send(far, far, other_core))
    for h, term in enumerate(diags.end()):
        out_d[:, :, halves[h]] = cd[:, :, halves[h]] - term
    cross.wait_recv()
    out_b[...] = cb[...] - (b_keep[...] + b_in[...])
    for copy in core_backs:
        copy.wait_recv()
    out_f[...] = cf[...] - full[...]
    net.drain()


def exchange(first, band, diag, c_first, c_band, c_diag):
    w = first.shape[0]
    half = w // 2
    sub, drow, k = band.shape[0] // 8, diag.shape[1] // 8, diag.shape[0]
    zrow = half // 4
    yrow = zrow // 4
    vmem, hbm = pl.BlockSpec(memory_space=pltpu.VMEM), pl.BlockSpec(memory_space=pl.ANY)
    v = lambda *shape: pltpu.VMEM(shape, F32)
    return pl.pallas_call(
        exchange_kernel,
        out_shape=tuple(jax.ShapeDtypeStruct(a.shape, F32) for a in (c_first, c_band, c_diag)),
        in_specs=[vmem] * 3 + [hbm] * 3,
        out_specs=(vmem, vmem, vmem),
        scratch_shapes=[
            v(*c_first.shape), v(*c_band.shape), v(*c_diag.shape),
            v(half, w), v(half, w), v(2, zrow, half), v(2, zrow, half), v(2, 2, zrow, half), v(zrow, w),
            v(3, yrow, w), v(4, yrow, w), v(w, w),
            v(2, 2, sub, half), v(2, 2, sub, half), v(2, 2, 2, sub, half), v(sub, w), v(sub, w), v(sub, w),
            v(4, k, drow, w), v(2, k, drow, half), v(2, k, drow, half), v(2, 2, k, drow, half),
            pltpu.SemaphoreType.DMA((64,)), pltpu.SemaphoreType.DMA((64,)), pltpu.SemaphoreType.DMA((3,)),
        ],
        compiler_params=pltpu.CompilerParams(
            vmem_limit_bytes=32 << 20, collective_id=0, has_side_effects=True
        ),
        name="exchange",
    )(first, band, diag, c_first, c_band, c_diag)


def shards(counts, blocks, factors, b_first, b_branch, c_first, c_band, c_diag):
    first, band, diag = local_sums(counts, blocks, factors, b_first, b_branch, c_diag.shape[0])
    return exchange(first, band.reshape(-1, band.shape[-1]), diag, c_first, c_band, c_diag)


def solution(mesh):
    placed = (
        P(("branch", "scen")),
        P(("branch", "scen")),
        P(("branch", "scen"), None, None),
        P(("branch", "scen"), None, None),
        P(("branch", "scen"), None, None),
        P(),
        P(("branch", "scen"), None),
        P("branch", "scen", None),
    )
    return jax.shard_map(
        shards,
        mesh=mesh,
        in_specs=placed,
        out_specs=(P(), P(("branch", "scen"), None), P("branch", "scen", None)),
        check_vma=False,
    )
```

```python
import jax
import jax.numpy as jnp
from jax import lax
from jax.experimental import pallas as pl
from jax.experimental.pallas import tpu as pltpu
from jax.sharding import PartitionSpec as P

F32, BF16 = jnp.float32, jnp.bfloat16


def split(value):
    high = value.astype(BF16)
    return high, (value - high.astype(F32)).astype(BF16)


def dot3(left, right, dims):
    (lh, ll), (rh, rl) = left, right
    one = lambda a, b: lax.dot_general(a, b, (dims, ((), ())), preferred_element_type=F32)
    return one(lh, rl) + one(ll, rh) + one(lh, rh)


NN = ((1,), (0,))
TN = ((0,), (0,))


def on_diagonal(wide):
    lane = lax.broadcasted_iota(jnp.int32, wide.shape, 1)
    left = lane < wide.shape[0]
    zero = jnp.zeros_like(wide)
    return jnp.concatenate([jnp.where(left, wide, zero), jnp.where(left, zero, wide)], axis=0)


def dot1(left, right):
    return lax.dot_general(left.astype(BF16), right.astype(BF16), (NN, ((), ())), preferred_element_type=F32)


def pair_inverses(wides):
    rows, cols = wides[0].shape
    r = lax.broadcasted_iota(jnp.int32, (rows, cols), 0)
    c = lax.broadcasted_iota(jnp.int32, (rows, cols), 1) & (rows - 1)
    eye = r == c
    out = []
    for wide in wides:
        pivots = jnp.where(eye, wide, 0.0)
        by_col = 1.0 / jnp.sum(pivots, axis=0, keepdims=True)
        by_row = 1.0 / jnp.concatenate(
            [
                jnp.broadcast_to(jnp.sum(pivots[:, i : i + rows], axis=1, keepdims=True), (rows, rows))
                for i in range(0, cols, rows)
            ],
            axis=1,
        )
        pairs = ((r >> 1) == (c >> 1)) & (r > c)
        out.append(jnp.where(eye, by_row, 0.0) - jnp.where(pairs, wide * by_col * by_row, 0.0))
    shift = 1
    while (1 << shift) < rows:
        below = ((r >> (shift + 1)) == (c >> (shift + 1))) & ((r >> shift) > (c >> shift))
        mids = [dot1(jnp.where(below, w, 0.0), on_diagonal(x)) for w, x in zip(wides, out)]
        out = [x - dot1(x, on_diagonal(m)) for x, m in zip(out, mids)]
        shift += 1
    unit = jnp.where(eye, 1.0, 0.0)
    for _ in range(NEWTON):
        errs = [unit - dot3(split(w), split(on_diagonal(x)), NN) for w, x in zip(wides, out)]
        out = [x + dot1(x, on_diagonal(e)) for x, e in zip(out, errs)]
    return out


NEWTON = 2


def invert(fac, inv_h, inv_l, slots):
    n = fac.shape[1]
    half, q = n // 2, n // 4
    wides = []
    for s in slots:
        for o in (0, half):
            wides.append(
                jnp.concatenate([fac[s, o : o + q, o : o + q], fac[s, o + q : o + half, o + q : o + half]], axis=1)
            )
    invs = pair_inverses(wides)
    parts = [(split(w[:, :q]), split(w[:, q:])) for w in invs]
    lows = [
        dot3(split(fac[s, o + q : o + half, o : o + q]), parts[2 * i + j][0], NN)
        for i, s in enumerate(slots)
        for j, o in enumerate((0, half))
    ]
    corners = [split(-dot3(p[1], split(m), NN)) for p, m in zip(parts, lows)]
    zero = jnp.zeros((q, q), BF16)
    for i, s in enumerate(slots):
        for j, o in enumerate((0, half)):
            (a, d), corner = parts[2 * i + j], corners[2 * i + j]
            for h, ref in enumerate((inv_h, inv_l)):
                ref[s, o : o + q, o : o + q] = a[h]
                ref[s, o : o + q, o + q : o + half] = zero
                ref[s, o + q : o + half, o : o + q] = corner[h]
                ref[s, o + q : o + half, o + q : o + half] = d[h]
    lows = [
        dot3(split(fac[s, half:, :half]), (inv_h[s, :half, :half], inv_l[s, :half, :half]), NN) for s in slots
    ]
    for s, low in zip(slots, lows):
        corner = -dot3((inv_h[s, half:, half:], inv_l[s, half:, half:]), split(low), NN)
        inv_h[s, half:, :half], inv_l[s, half:, :half] = split(corner)


def compute_kernel(counts, blocks, fac_hbm, bf_hbm, bb_hbm, first, band, diag, fac, rhs, inv_h, inv_l, yh, yl, sems):
    n, w = fac_hbm.shape[1], bf_hbm.shape[2]
    cap = fac_hbm.shape[0]
    half = n // 2
    live = counts[0]
    fac_loads = [pltpu.make_async_copy(fac_hbm.at[s], fac.at[s], sems.at[s, 0]) for s in range(cap)]
    rhs_loads = [
        (
            pltpu.make_async_copy(bf_hbm.at[s], rhs.at[s, :, pl.ds(0, w)], sems.at[s, 1]),
            pltpu.make_async_copy(bb_hbm.at[s], rhs.at[s, :, pl.ds(w, w)], sems.at[s, 2]),
        )
        for s in range(cap)
    ]
    for copy in fac_loads:
        copy.start()
    for pair in rhs_loads:
        for copy in pair:
            copy.start()
    first[...] = jnp.zeros_like(first)
    band[...] = jnp.zeros_like(band)
    diag[...] = jnp.zeros_like(diag)
    for copy in fac_loads:
        copy.wait()
    for g in range(0, cap, GROUP):
        invert(fac, inv_h, inv_l, range(g, g + GROUP))
    for pair in rhs_loads:
        for copy in pair:
            copy.wait()

    @pl.loop(0, live)
    def _(s):
        top = (inv_h[s, :half, :half], inv_l[s, :half, :half])
        low = (inv_h[s, half:, :], inv_l[s, half:, :])
        for col in range(0, 2 * w, half):
            cols = pl.ds(col, half)
            right = split(rhs[s, :, cols])
            yh[:half, cols], yl[:half, cols] = split(dot3(top, (right[0][:half], right[1][:half]), NN))
            yh[half:, cols], yl[half:, cols] = split(dot3(low, right, NN))
        k = blocks[s] & 1
        for i in range(0, 2 * w, half):
            left = (yh[:, pl.ds(i, half)], yl[:, pl.ds(i, half)])
            for j in range(0, i + half, half):
                right = (yh[:, pl.ds(j, half)], yl[:, pl.ds(j, half)])
                term = dot3(left, right, TN)
                if i < w:
                    first[pl.ds(i, half), pl.ds(j, half)] += term
                elif j < w:
                    band[k, pl.ds(i - w, half), pl.ds(j, half)] += term
                else:
                    diag[k, pl.ds(i - w, half), pl.ds(j - w, half)] += term

    first[:half, half:] = first[half:, :half].T
    for k in range(diag.shape[0]):
        diag[k, :half, half:] = diag[k, half:, :half].T


GROUP = 4


def local_sums(counts, blocks, factors, b_first, b_branch, block_count):
    cap, n, w = b_first.shape
    smem = pl.BlockSpec(memory_space=pltpu.SMEM)
    hbm = pl.BlockSpec(memory_space=pl.ANY)
    vmem = pl.BlockSpec(memory_space=pltpu.VMEM)
    return pl.pallas_call(
        compute_kernel,
        out_shape=(
            jax.ShapeDtypeStruct((w, w), F32),
            jax.ShapeDtypeStruct((block_count, w, w), F32),
            jax.ShapeDtypeStruct((block_count, w, w), F32),
        ),
        in_specs=[smem, smem, hbm, hbm, hbm],
        out_specs=(vmem, vmem, vmem),
        scratch_shapes=[
            pltpu.VMEM((cap, n, n), F32),
            pltpu.VMEM((cap, n, 2 * w), F32),
            pltpu.VMEM((cap, n, n), BF16),
            pltpu.VMEM((cap, n, n), BF16),
            pltpu.VMEM((n, 2 * w), BF16),
            pltpu.VMEM((n, 2 * w), BF16),
            pltpu.SemaphoreType.DMA((cap, 3)),
        ],
        compiler_params=pltpu.CompilerParams(vmem_limit_bytes=48 << 20),
        name="local_sums",
    )(counts, blocks, factors, b_first, b_branch)


class Net:
    def __init__(self, send_sems, recv_sems):
        self.sems = (send_sems, recv_sems)
        self.count = 0
        self.sent = []

    def send(self, source, target, device):
        copy = pltpu.make_async_remote_copy(
            src_ref=source,
            dst_ref=target,
            send_sem=self.sems[0].at[self.count],
            recv_sem=self.sems[1].at[self.count],
            device_id=device,
            device_id_type=pl.DeviceIdType.MESH,
        )
        copy.start()
        self.count += 1
        self.sent.append(copy)
        return copy

    def drain(self):
        for copy in self.sent:
            copy.wait_send()


FAR, NEXT, PREV, OWN = 0, 1, 2, 3
OFFSETS = (2, 1, 3, 0)


class Ring:
    def __init__(self, net, piece, up, down, far_in, out, near_in):
        self.net, self.piece, self.up, self.down = net, piece, up, down
        self.far_in, self.out, self.near_in = far_in, out, near_in

    def far(self):
        self.far_up = self.net.send(self.piece(FAR, 0), self.far_in.at[0], self.up)
        self.far_down = self.net.send(self.piece(FAR, 1), self.far_in.at[1], self.down)

    def near_up(self):
        self.n01 = self.net.send(self.piece(NEXT, 1), self.near_in.at[0, 1], self.up)

    def near_down(self):
        self.n10 = self.net.send(self.piece(PREV, 0), self.near_in.at[1, 0], self.down)

    def mid_up(self):
        self.far_up.wait_recv()
        self.out[0] = self.piece(NEXT, 0)[...] + self.far_in[0]
        self.n00 = self.net.send(self.out.at[0], self.near_in.at[0, 0], self.up)

    def mid_down(self):
        self.far_down.wait_recv()
        self.out[1] = self.piece(PREV, 1)[...] + self.far_in[1]
        self.n11 = self.net.send(self.out.at[1], self.near_in.at[1, 1], self.down)

    def end(self):
        for copy in (self.n01, self.n10, self.n00, self.n11):
            copy.wait_recv()
        return [self.piece(OWN, h)[...] + self.near_in[0, h] + self.near_in[1, h] for h in range(2)]


def exchange_kernel(
    first, band, diag, cf_hbm, cb_hbm, cd_hbm, out_f, out_b, out_d,
    cf, cb, cd, core_in, held, z_far, z_out, z_near, z_sum, y_in, x_all, full,
    b_far, b_out, b_near, b_send, b_in, b_keep, d_in, d_far, d_out, d_near, send_sems, recv_sems, c_sems,
):
    b, s = lax.axis_index("branch"), lax.axis_index("scen")
    z, y_hi, core = b // 4, (b // 2) % 2, b % 2
    x, y_lo = s // 2, s % 2
    y = 2 * y_hi + y_lo
    w = first.shape[1]
    half = w // 2
    halves = (pl.ds(0, half), pl.ds(half, half))
    net = Net(send_sems, recv_sems)

    other_core = (b + 1 - 2 * core, s)
    z_up, z_down = (((z + 1) % 4) * 4 + b % 4, s), (((z + 3) % 4) * 4 + b % 4, s)
    y_peers = []
    for d in (1, 2, 3):
        there = (y + d) % 4
        y_peers.append((z * 4 + (there // 2) * 2 + core, x * 2 + there % 2))
    x_peers = [(b, ((x + d) % 4) * 2 + y_lo) for d in (1, 2, 3)]
    x_up, x_down = x_peers[0], x_peers[2]
    y_near = (b, x * 2 + 1 - y_lo)

    c_copies = [
        pltpu.make_async_copy(source, target, c_sems.at[i])
        for i, (source, target) in enumerate(((cf_hbm, cf), (cb_hbm, cb), (cd_hbm, cd)))
    ]
    for copy in c_copies:
        copy.start()

    barrier = pltpu.get_barrier_semaphore()
    greeted = [other_core, z_up, z_down] + y_peers + x_peers
    for peer in greeted:
        pl.semaphore_signal(barrier, inc=1, device_id=peer, device_id_type=pl.DeviceIdType.MESH)
    pl.semaphore_wait(barrier, len(greeted))

    rows_core = pl.multiple_of(core * half, half)
    core_rows, core_far = pl.ds(rows_core, half), pl.ds(pl.multiple_of((1 - core) * half, half), half)
    core_copy = net.send(first.at[core_far], core_in, other_core)

    sub = band.shape[0] // 8
    bands = []
    for chunk, y_to in enumerate((1 - y_lo, y_lo)):

        def band_piece(role, h, y_to=y_to):
            start = ((x + OFFSETS[role]) % 4) * (2 * sub) + y_to * sub
            return band.at[pl.ds(pl.multiple_of(start, sub), sub), halves[h]]

        bands.append(Ring(net, band_piece, x_up, x_down, b_far.at[chunk], b_out.at[chunk], b_near.at[chunk]))
    drow = diag.shape[1] // 8

    def diag_rows(role, y_to):
        start = ((x + OFFSETS[role]) % 4) * (2 * drow) + y_to * drow
        return diag.at[:, pl.ds(pl.multiple_of(start, drow), drow), :]

    def diag_send(role):
        return net.send(diag_rows(role, 1 - y_lo), d_in.at[role], y_near)

    def diag_take(copy, role):
        copy.wait_recv()
        d_in[role] += diag_rows(role, y_lo)[...]

    diags = Ring(net, lambda role, h: d_in.at[role, :, :, halves[h]], x_up, x_down, d_far, d_out, d_near)

    zrow = half // 4
    z_ring = Ring(
        net,
        lambda role, h: held.at[pl.ds(pl.multiple_of(((z + OFFSETS[role]) % 4) * zrow, zrow), zrow), halves[h]],
        z_up, z_down, z_far, z_out, z_near,
    )

    bands[0].far()
    d0 = diag_send(FAR)
    bands[1].far()
    bands[0].near_up()
    bands[0].near_down()

    core_copy.wait_recv()
    held[...] = first[core_rows] + core_in[...]
    z_ring.far()
    z_ring.near_up()
    z_ring.near_down()
    d1 = diag_send(NEXT)
    bands[0].mid_up()
    bands[0].mid_down()
    z_ring.mid_up()
    z_ring.mid_down()
    diag_take(d0, FAR)
    diags.far()

    z_sum[:, :half], z_sum[:, half:] = z_ring.end()
    yrow = zrow // 4
    y_copies = []
    for d in (1, 2, 3):
        piece = z_sum.at[pl.ds(pl.multiple_of(((y + d) % 4) * yrow, yrow), yrow)]
        y_copies.append(net.send(piece, y_in.at[d - 1], y_peers[d - 1]))
    d2 = diag_send(PREV)
    bands[1].mid_up()
    bands[1].mid_down()
    for copy in y_copies:
        copy.wait_recv()
    own = z_sum[pl.ds(pl.multiple_of(y * yrow, yrow), yrow)]
    x_all[x] = own + y_in[0] + y_in[1] + y_in[2]
    x_copies = [net.send(x_all.at[x], x_all.at[x], peer) for peer in x_peers]
    bands[1].near_up()
    bands[1].near_down()
    diag_take(d1, NEXT)
    diags.near_up()
    diags.mid_up()

    for copy in x_copies:
        copy.wait_recv()
    z_rows = rows_core + z * zrow
    y_rows = pl.ds(pl.multiple_of(z_rows + y * yrow, yrow), yrow)
    full[y_rows] = (x_all[0] + x_all[1]) + (x_all[2] + x_all[3])
    y_back = [net.send(full.at[y_rows], full.at[y_rows], peer) for peer in y_peers]
    d3 = diag_send(OWN)
    b_send[:, :half], b_send[:, half:] = bands[0].end()
    cross = net.send(b_send, b_in, y_near)
    diag_take(d2, PREV)
    diags.near_down()
    diags.mid_down()

    for copy in y_back:
        copy.wait_recv()

    def z_block(offset):
        return pl.ds(pl.multiple_of(rows_core + ((z + offset) % 4) * zrow, zrow), zrow)

    mine = full.at[z_block(0)]
    up_copy, down_copy = net.send(mine, mine, z_up), net.send(mine, mine, z_down)
    core_backs = [net.send(mine, mine, other_core)]
    b_keep[:, :half], b_keep[:, half:] = bands[1].end()
    up_copy.wait_recv()
    below = full.at[z_block(3)]
    pass_up = net.send(full.at[z_block(3), halves[0]], full.at[z_block(3), halves[0]], z_up)
    core_backs.append(net.send(below, below, other_core))
    down_copy.wait_recv()
    above = full.at[z_block(1)]
    pass_down = net.send(full.at[z_block(1), halves[1]], full.at[z_block(1), halves[1]], z_down)
    core_backs.append(net.send(above, above, other_core))
    for copy in c_copies:
        copy.wait()
    diag_take(d3, OWN)
    pass_up.wait_recv()
    pass_down.wait_recv()
    far = full.at[z_block(2)]
    core_backs.append(net.send(far, far, other_core))
    for h, term in enumerate(diags.end()):
        out_d[:, :, halves[h]] = cd[:, :, halves[h]] - term
    cross.wait_recv()
    out_b[...] = cb[...] - (b_keep[...] + b_in[...])
    for copy in core_backs:
        copy.wait_recv()
    out_f[...] = cf[...] - full[...]
    net.drain()


def exchange(first, band, diag, c_first, c_band, c_diag):
    w = first.shape[0]
    half = w // 2
    sub, drow, k = band.shape[0] // 8, diag.shape[1] // 8, diag.shape[0]
    zrow = half // 4
    yrow = zrow // 4
    vmem, hbm = pl.BlockSpec(memory_space=pltpu.VMEM), pl.BlockSpec(memory_space=pl.ANY)
    v = lambda *shape: pltpu.VMEM(shape, F32)
    return pl.pallas_call(
        exchange_kernel,
        out_shape=tuple(jax.ShapeDtypeStruct(a.shape, F32) for a in (c_first, c_band, c_diag)),
        in_specs=[vmem] * 3 + [hbm] * 3,
        out_specs=(vmem, vmem, vmem),
        scratch_shapes=[
            v(*c_first.shape), v(*c_band.shape), v(*c_diag.shape),
            v(half, w), v(half, w), v(2, zrow, half), v(2, zrow, half), v(2, 2, zrow, half), v(zrow, w),
            v(3, yrow, w), v(4, yrow, w), v(w, w),
            v(2, 2, sub, half), v(2, 2, sub, half), v(2, 2, 2, sub, half), v(sub, w), v(sub, w), v(sub, w),
            v(4, k, drow, w), v(2, k, drow, half), v(2, k, drow, half), v(2, 2, k, drow, half),
            pltpu.SemaphoreType.DMA((64,)), pltpu.SemaphoreType.DMA((64,)), pltpu.SemaphoreType.DMA((3,)),
        ],
        compiler_params=pltpu.CompilerParams(
            vmem_limit_bytes=32 << 20, collective_id=0, has_side_effects=True
        ),
        name="exchange",
    )(first, band, diag, c_first, c_band, c_diag)


def shards(counts, blocks, factors, b_first, b_branch, c_first, c_band, c_diag):
    first, band, diag = local_sums(counts, blocks, factors, b_first, b_branch, c_diag.shape[0])
    return exchange(first, band.reshape(-1, band.shape[-1]), diag, c_first, c_band, c_diag)


def solution(mesh):
    placed = (
        P(("branch", "scen")),
        P(("branch", "scen")),
        P(("branch", "scen"), None, None),
        P(("branch", "scen"), None, None),
        P(("branch", "scen"), None, None),
        P(),
        P(("branch", "scen"), None),
        P("branch", "scen", None),
    )
    return jax.shard_map(
        shards,
        mesh=mesh,
        in_specs=placed,
        out_specs=(P(), P(("branch", "scen"), None), P("branch", "scen", None)),
        check_vma=False,
    )
```

```python
import jax
import jax.numpy as jnp
from jax import lax
from jax.experimental import pallas as pl
from jax.experimental.pallas import tpu as pltpu
from jax.sharding import PartitionSpec as P

F32, BF16 = jnp.float32, jnp.bfloat16


def split(value):
    high = value.astype(BF16)
    return high, (value - high.astype(F32)).astype(BF16)


def dot3(left, right, dims):
    (lh, ll), (rh, rl) = left, right
    one = lambda a, b: lax.dot_general(a, b, (dims, ((), ())), preferred_element_type=F32)
    return one(lh, rl) + one(ll, rh) + one(lh, rh)


NN = ((1,), (0,))
TN = ((0,), (0,))


def on_diagonal(wide):
    lane = lax.broadcasted_iota(jnp.int32, wide.shape, 1)
    left = lane < wide.shape[0]
    zero = jnp.zeros_like(wide)
    return jnp.concatenate([jnp.where(left, wide, zero), jnp.where(left, zero, wide)], axis=0)


def dot1(left, right):
    return lax.dot_general(left.astype(BF16), right.astype(BF16), (NN, ((), ())), preferred_element_type=F32)


def pair_inverses(wides):
    rows, cols = wides[0].shape
    r = lax.broadcasted_iota(jnp.int32, (rows, cols), 0)
    c = lax.broadcasted_iota(jnp.int32, (rows, cols), 1) & (rows - 1)
    eye = r == c
    out = []
    for wide in wides:
        pivots = jnp.where(eye, wide, 0.0)
        by_col = 1.0 / jnp.sum(pivots, axis=0, keepdims=True)
        by_row = 1.0 / jnp.concatenate(
            [
                jnp.broadcast_to(jnp.sum(pivots[:, i : i + rows], axis=1, keepdims=True), (rows, rows))
                for i in range(0, cols, rows)
            ],
            axis=1,
        )
        pairs = ((r >> 1) == (c >> 1)) & (r > c)
        out.append(jnp.where(eye, by_row, 0.0) - jnp.where(pairs, wide * by_col * by_row, 0.0))
    shift = 1
    while (1 << shift) < rows:
        below = ((r >> (shift + 1)) == (c >> (shift + 1))) & ((r >> shift) > (c >> shift))
        mids = [dot1(jnp.where(below, w, 0.0), on_diagonal(x)) for w, x in zip(wides, out)]
        out = [x - dot1(x, on_diagonal(m)) for x, m in zip(out, mids)]
        shift += 1
    unit = jnp.where(eye, 1.0, 0.0)
    for _ in range(NEWTON):
        errs = [unit - dot3(split(w), split(on_diagonal(x)), NN) for w, x in zip(wides, out)]
        out = [x + dot1(x, on_diagonal(e)) for x, e in zip(out, errs)]
    return out


NEWTON = 2


def invert(fac, inv_h, inv_l, slots):
    n = fac.shape[1]
    half, q = n // 2, n // 4
    wides = []
    for s in slots:
        for o in (0, half):
            wides.append(
                jnp.concatenate([fac[s, o : o + q, o : o + q], fac[s, o + q : o + half, o + q : o + half]], axis=1)
            )
    invs = pair_inverses(wides)
    parts = [(split(w[:, :q]), split(w[:, q:])) for w in invs]
    lows = [
        dot3(split(fac[s, o + q : o + half, o : o + q]), parts[2 * i + j][0], NN)
        for i, s in enumerate(slots)
        for j, o in enumerate((0, half))
    ]
    corners = [split(-dot3(p[1], split(m), NN)) for p, m in zip(parts, lows)]
    zero = jnp.zeros((q, q), BF16)
    for i, s in enumerate(slots):
        for j, o in enumerate((0, half)):
            (a, d), corner = parts[2 * i + j], corners[2 * i + j]
            for h, ref in enumerate((inv_h, inv_l)):
                ref[s, o : o + q, o : o + q] = a[h]
                ref[s, o : o + q, o + q : o + half] = zero
                ref[s, o + q : o + half, o : o + q] = corner[h]
                ref[s, o + q : o + half, o + q : o + half] = d[h]
    lows = [
        dot3(split(fac[s, half:, :half]), (inv_h[s, :half, :half], inv_l[s, :half, :half]), NN) for s in slots
    ]
    for s, low in zip(slots, lows):
        corner = -dot3((inv_h[s, half:, half:], inv_l[s, half:, half:]), split(low), NN)
        inv_h[s, half:, :half], inv_l[s, half:, :half] = split(corner)


class Net:
    def __init__(self, send_sems, recv_sems):
        self.sems = (send_sems, recv_sems)
        self.count = 0
        self.sent = []

    def send(self, source, target, device):
        copy = pltpu.make_async_remote_copy(
            src_ref=source,
            dst_ref=target,
            send_sem=self.sems[0].at[self.count],
            recv_sem=self.sems[1].at[self.count],
            device_id=device,
            device_id_type=pl.DeviceIdType.MESH,
        )
        copy.start()
        self.count += 1
        self.sent.append(copy)
        return copy

    def drain(self):
        for copy in self.sent:
            copy.wait_send()


FAR, NEXT, PREV, OWN = 0, 1, 2, 3
OFFSETS = (2, 1, 3, 0)


class Ring:
    def __init__(self, net, piece, up, down, far_in, out, near_in):
        self.net, self.piece, self.up, self.down = net, piece, up, down
        self.far_in, self.out, self.near_in = far_in, out, near_in

    def far(self):
        self.far_up = self.net.send(self.piece(FAR, 0), self.far_in.at[0], self.up)
        self.far_down = self.net.send(self.piece(FAR, 1), self.far_in.at[1], self.down)

    def near_up(self):
        self.n01 = self.net.send(self.piece(NEXT, 1), self.near_in.at[0, 1], self.up)

    def near_down(self):
        self.n10 = self.net.send(self.piece(PREV, 0), self.near_in.at[1, 0], self.down)

    def mid_up(self):
        self.far_up.wait_recv()
        self.out[0] = self.piece(NEXT, 0)[...] + self.far_in[0]
        self.n00 = self.net.send(self.out.at[0], self.near_in.at[0, 0], self.up)

    def mid_down(self):
        self.far_down.wait_recv()
        self.out[1] = self.piece(PREV, 1)[...] + self.far_in[1]
        self.n11 = self.net.send(self.out.at[1], self.near_in.at[1, 1], self.down)

    def end(self):
        for copy in (self.n01, self.n10, self.n00, self.n11):
            copy.wait_recv()
        return [self.piece(OWN, h)[...] + self.near_in[0, h] + self.near_in[1, h] for h in range(2)]


def fused_kernel(
    counts, blocks, fac_hbm, bf_hbm, bb_hbm, out_f, out_b, out_d,
    fac, rhs, inv_h, inv_l, y0_h, y0_l, y1_h, y1_l, first, band, diag,
    core_in, held, z_far, z_out, z_near, z_sum, y_in, x_all, full,
    b_far, b_out, b_near, b_send, b_in, b_keep, d_in, d_far, d_out, d_near,
    load_sems, send_sems, recv_sems,
):
    b, s = lax.axis_index("branch"), lax.axis_index("scen")
    z, y_hi, core = b // 4, (b // 2) % 2, b % 2
    x, y_lo = s // 2, s % 2
    y = 2 * y_hi + y_lo
    cap, n, w = bf_hbm.shape
    half = w // 2
    halves = (pl.ds(0, half), pl.ds(half, half))
    net = Net(send_sems, recv_sems)

    fac_loads = [pltpu.make_async_copy(fac_hbm.at[t], fac.at[t], load_sems.at[t]) for t in range(cap)]
    rest = []
    for t in range(cap):
        rest.append((bf_hbm.at[t], rhs.at[t, :, pl.ds(0, w)]))
        rest.append((bb_hbm.at[t], rhs.at[t, :, pl.ds(w, w)]))
    rest_loads = [pltpu.make_async_copy(a, c, load_sems.at[cap + i]) for i, (a, c) in enumerate(rest)]
    for copy in fac_loads + rest_loads:
        copy.start()

    other_core = (b + 1 - 2 * core, s)
    z_up, z_down = (((z + 1) % 4) * 4 + b % 4, s), (((z + 3) % 4) * 4 + b % 4, s)
    y_peers = []
    for d in (1, 2, 3):
        there = (y + d) % 4
        y_peers.append((z * 4 + (there // 2) * 2 + core, x * 2 + there % 2))
    x_peers = [(b, ((x + d) % 4) * 2 + y_lo) for d in (1, 2, 3)]
    x_up, x_down = x_peers[0], x_peers[2]
    y_near = (b, x * 2 + 1 - y_lo)
    barrier = pltpu.get_barrier_semaphore()
    greeted = [other_core, z_up, z_down] + y_peers + x_peers
    for peer in greeted:
        pl.semaphore_signal(barrier, inc=1, device_id=peer, device_id_type=pl.DeviceIdType.MESH)

    for copy in fac_loads:
        copy.wait()
    invert(fac, inv_h, inv_l, range(cap))
    for copy in rest_loads:
        copy.wait()

    first[...] = jnp.zeros_like(first)

    def chosen(t, shape):
        return jnp.broadcast_to(jnp.where(t < counts[0], blocks[t] % 2, 2), shape)

    def solve(t, start, y_h, y_l):
        top = (inv_h[t, :half, :half], inv_l[t, :half, :half])
        low = (inv_h[t, half:, :], inv_l[t, half:, :])
        live = chosen(t, (half, half)) < 2
        for cols in halves:
            right = split(rhs[t, :, pl.ds(start + cols.start, half)])
            up = dot3(top, (right[0][:half], right[1][:half]), NN)
            y_h[t, :half, cols], y_l[t, :half, cols] = split(jnp.where(live, up, 0.0))
            down = dot3(low, right, NN)
            y_h[t, half:, cols], y_l[t, half:, cols] = split(jnp.where(live, down, 0.0))

    @pl.loop(0, cap)
    def _(t):
        solve(t, 0, y0_h, y0_l)
        for i in range(0, w, half):
            left = (y0_h[t, :, pl.ds(i, half)], y0_l[t, :, pl.ds(i, half)])
            for j in range(0, i + half, half):
                right = (y0_h[t, :, pl.ds(j, half)], y0_l[t, :, pl.ds(j, half)])
                first[pl.ds(i, half), pl.ds(j, half)] += dot3(left, right, TN)

    first[:half, half:] = first[half:, :half].T

    pl.semaphore_wait(barrier, len(greeted))
    rows_core = pl.multiple_of(core * half, half)
    core_rows, core_far = pl.ds(rows_core, half), pl.ds(pl.multiple_of((1 - core) * half, half), half)
    core_copy = net.send(first.at[core_far], core_in, other_core)

    @pl.loop(0, cap)
    def _(t):
        solve(t, w, y1_h, y1_l)

    quarter = half // 2

    def place(role):
        return (x + OFFSETS[role]) % 4

    def band_terms(pair):
        cols = pl.ds(pl.multiple_of((place(pair[0]) % 2) * half, half), half)
        for role in pair:
            band[role] = jnp.zeros((half, w), F32)

        @pl.loop(0, cap)
        def _(t):
            which = chosen(t, (half, w))
            term = dot3((y1_h[t, :, cols], y1_l[t, :, cols]), (y0_h[t], y0_l[t]), TN)
            for role in pair:
                band[role] += jnp.where(which == place(role) // 2, term, 0.0)

    def diag_terms(pair):
        cols = [pl.ds(pl.multiple_of(place(role) * quarter, quarter), quarter) for role in pair]
        for role in pair:
            diag[role] = jnp.zeros((half, w), F32)

        @pl.loop(0, cap)
        def _(t):
            which = chosen(t, (quarter, w))
            left = [jnp.concatenate([y[t, :, c] for c in cols], axis=1) for y in (y1_h, y1_l)]
            term = dot3(left, (y1_h[t], y1_l[t]), TN)
            for i, role in enumerate(pair):
                for k in range(2):
                    part = jnp.where(which == k, term[i * quarter : (i + 1) * quarter], 0.0)
                    diag[role, pl.ds(k * quarter, quarter)] += part

    sub, drow = half // 2, quarter // 2
    bands = []
    for chunk, y_to in enumerate((1 - y_lo, y_lo)):

        def band_piece(role, h, y_to=y_to):
            return band.at[role, pl.ds(pl.multiple_of(y_to * sub, sub), sub), halves[h]]

        bands.append(Ring(net, band_piece, x_up, x_down, b_far.at[chunk], b_out.at[chunk], b_near.at[chunk]))

    def diag_rows(role, k, y_to):
        return diag.at[role, pl.ds(pl.multiple_of(k * quarter + y_to * drow, drow), drow), :]

    def diag_send(role):
        return [net.send(diag_rows(role, k, 1 - y_lo), d_in.at[role, k], y_near) for k in range(2)]

    def diag_take(copies, role):
        for k, copy in enumerate(copies):
            copy.wait_recv()
            d_in[role, k] += diag_rows(role, k, y_lo)[...]

    diags = Ring(net, lambda role, h: d_in.at[role, :, :, halves[h]], x_up, x_down, d_far, d_out, d_near)

    zrow = half // 4
    z_ring = Ring(
        net,
        lambda role, h: held.at[pl.ds(pl.multiple_of(((z + OFFSETS[role]) % 4) * zrow, zrow), zrow), halves[h]],
        z_up, z_down, z_far, z_out, z_near,
    )

    core_copy.wait_recv()
    held[...] = first[core_rows] + core_in[...]
    z_ring.far()
    z_ring.near_up()
    z_ring.near_down()
    diag_terms((FAR, OWN))
    d0 = diag_send(FAR)
    z_ring.mid_up()
    z_ring.mid_down()
    band_terms((FAR, OWN))
    bands[0].far()
    bands[1].far()
    diag_terms((NEXT, PREV))
    z_sum[:, :half], z_sum[:, half:] = z_ring.end()
    yrow = zrow // 4
    y_copies = []
    for d in (1, 2, 3):
        piece = z_sum.at[pl.ds(pl.multiple_of(((y + d) % 4) * yrow, yrow), yrow)]
        y_copies.append(net.send(piece, y_in.at[d - 1], y_peers[d - 1]))
    d1 = diag_send(NEXT)
    band_terms((NEXT, PREV))
    bands[0].near_up()
    bands[0].near_down()
    for copy in y_copies:
        copy.wait_recv()
    own = z_sum[pl.ds(pl.multiple_of(y * yrow, yrow), yrow)]
    x_all[x] = own + y_in[0] + y_in[1] + y_in[2]
    x_copies = [net.send(x_all.at[x], x_all.at[x], peer) for peer in x_peers]
    d2 = diag_send(PREV)
    bands[0].mid_up()
    bands[0].mid_down()
    diag_take(d0, FAR)
    diags.far()
    bands[1].near_up()
    bands[1].near_down()
    for copy in x_copies:
        copy.wait_recv()
    z_rows = rows_core + z * zrow
    y_rows = pl.ds(pl.multiple_of(z_rows + y * yrow, yrow), yrow)
    full[y_rows] = (x_all[0] + x_all[1]) + (x_all[2] + x_all[3])
    y_back = [net.send(full.at[y_rows], full.at[y_rows], peer) for peer in y_peers]
    d3 = diag_send(OWN)
    bands[1].mid_up()
    bands[1].mid_down()
    diag_take(d1, NEXT)
    diags.near_up()
    diags.mid_up()
    b_send[:, :half], b_send[:, half:] = bands[0].end()
    cross = net.send(b_send, b_in, y_near)
    diag_take(d2, PREV)
    diags.near_down()
    diags.mid_down()

    for copy in y_back:
        copy.wait_recv()

    def z_block(offset):
        return pl.ds(pl.multiple_of(rows_core + ((z + offset) % 4) * zrow, zrow), zrow)

    mine = full.at[z_block(0)]
    up_copy, down_copy = net.send(mine, mine, z_up), net.send(mine, mine, z_down)
    core_backs = [net.send(mine, mine, other_core)]
    b_keep[:, :half], b_keep[:, half:] = bands[1].end()
    up_copy.wait_recv()
    below = full.at[z_block(3)]
    pass_up = net.send(full.at[z_block(3), halves[0]], full.at[z_block(3), halves[0]], z_up)
    core_backs.append(net.send(below, below, other_core))
    down_copy.wait_recv()
    above = full.at[z_block(1)]
    pass_down = net.send(full.at[z_block(1), halves[1]], full.at[z_block(1), halves[1]], z_down)
    core_backs.append(net.send(above, above, other_core))
    diag_take(d3, OWN)
    pass_up.wait_recv()
    pass_down.wait_recv()
    far = full.at[z_block(2)]
    core_backs.append(net.send(far, far, other_core))
    for h, term in enumerate(diags.end()):
        out_d[:, :, halves[h]] = term
    cross.wait_recv()
    out_b[...] = b_keep[...] + b_in[...]
    for copy in core_backs:
        copy.wait_recv()
    out_f[...] = full[...]
    net.drain()


def fused(counts, blocks, factors, b_first, b_branch, c_first, c_band, c_diag):
    cap, n, w = b_first.shape
    half = w // 2
    k, drow = c_diag.shape[0], c_diag.shape[1]
    sub = c_band.shape[0]
    zrow = half // 4
    yrow = zrow // 4
    smem, vmem = pl.BlockSpec(memory_space=pltpu.SMEM), pl.BlockSpec(memory_space=pltpu.VMEM)
    hbm = pl.BlockSpec(memory_space=HBM)
    v = lambda *shape: pltpu.VMEM(shape, F32)
    vb = lambda *shape: pltpu.VMEM(shape, BF16)
    return pl.pallas_call(
        fused_kernel,
        out_shape=tuple(jax.ShapeDtypeStruct(a.shape, F32) for a in (c_first, c_band, c_diag)),
        in_specs=[smem] * 2 + [hbm] * 3,
        out_specs=(vmem, vmem, vmem),
        scratch_shapes=[
            v(cap, n, n), v(cap, n, 2 * w), vb(cap, n, n), vb(cap, n, n),
            vb(cap, n, w), vb(cap, n, w), vb(cap, n, w), vb(cap, n, w),
            v(w, w), v(4, half, w), v(4, half, w),
            v(half, w), v(half, w), v(2, zrow, half), v(2, zrow, half), v(2, 2, zrow, half), v(zrow, w),
            v(3, yrow, w), v(4, yrow, w), v(w, w),
            v(2, 2, sub, half), v(2, 2, sub, half), v(2, 2, 2, sub, half), v(sub, w), v(sub, w), v(sub, w),
            v(4, k, drow, w), v(2, k, drow, half), v(2, k, drow, half), v(2, 2, k, drow, half),
            pltpu.SemaphoreType.DMA((3 * cap,)),
            pltpu.SemaphoreType.DMA((64,)), pltpu.SemaphoreType.DMA((64,)),
        ],
        compiler_params=pltpu.CompilerParams(vmem_limit_bytes=46 << 20, collective_id=0, has_side_effects=True),
        name="schur",
    )(counts, blocks, factors, b_first, b_branch)


HBM = pltpu.HBM


def shards(counts, blocks, factors, b_first, b_branch, c_first, c_band, c_diag):
    first, band, diag = fused(counts, blocks, factors, b_first, b_branch, c_first, c_band, c_diag)
    return c_first - first, c_band - band, c_diag - diag


def solution(mesh):
    placed = (
        P(("branch", "scen")),
        P(("branch", "scen")),
        P(("branch", "scen"), None, None),
        P(("branch", "scen"), None, None),
        P(("branch", "scen"), None, None),
        P(),
        P(("branch", "scen"), None),
        P("branch", "scen", None),
    )
    return jax.shard_map(
        shards,
        mesh=mesh,
        in_specs=placed,
        out_specs=(P(), P(("branch", "scen"), None), P("branch", "scen", None)),
        check_vma=False,
    )
```

```python
import jax
import jax.numpy as jnp
from jax import lax
from jax.experimental import pallas as pl
from jax.experimental.pallas import tpu as pltpu
from jax.sharding import PartitionSpec as P

F32, BF16 = jnp.float32, jnp.bfloat16


def split(value):
    high = value.astype(BF16)
    return high, (value - high.astype(F32)).astype(BF16)


def dot3(left, right, dims):
    (lh, ll), (rh, rl) = left, right
    one = lambda a, b: lax.dot_general(a, b, (dims, ((), ())), preferred_element_type=F32)
    return one(lh, rl) + one(ll, rh) + one(lh, rh)


NN = ((1,), (0,))
TN = ((0,), (0,))


def on_diagonal(wide):
    lane = lax.broadcasted_iota(jnp.int32, wide.shape, 1)
    left = lane < wide.shape[0]
    zero = jnp.zeros_like(wide)
    return jnp.concatenate([jnp.where(left, wide, zero), jnp.where(left, zero, wide)], axis=0)


def dot1(left, right):
    return lax.dot_general(left.astype(BF16), right.astype(BF16), (NN, ((), ())), preferred_element_type=F32)


def pair_inverses(wides):
    rows, cols = wides[0].shape
    r = lax.broadcasted_iota(jnp.int32, (rows, cols), 0)
    c = lax.broadcasted_iota(jnp.int32, (rows, cols), 1) & (rows - 1)
    eye = r == c
    out = []
    for wide in wides:
        pivots = jnp.where(eye, wide, 0.0)
        by_col = 1.0 / jnp.sum(pivots, axis=0, keepdims=True)
        by_row = 1.0 / jnp.concatenate(
            [
                jnp.broadcast_to(jnp.sum(pivots[:, i : i + rows], axis=1, keepdims=True), (rows, rows))
                for i in range(0, cols, rows)
            ],
            axis=1,
        )
        pairs = ((r >> 1) == (c >> 1)) & (r > c)
        out.append(jnp.where(eye, by_row, 0.0) - jnp.where(pairs, wide * by_col * by_row, 0.0))
    shift = 1
    while (1 << shift) < rows:
        below = ((r >> (shift + 1)) == (c >> (shift + 1))) & ((r >> shift) > (c >> shift))
        mids = [dot1(jnp.where(below, w, 0.0), on_diagonal(x)) for w, x in zip(wides, out)]
        out = [x - dot1(x, on_diagonal(m)) for x, m in zip(out, mids)]
        shift += 1
    unit = jnp.where(eye, 1.0, 0.0)
    for _ in range(NEWTON):
        errs = [unit - dot3(split(w), split(on_diagonal(x)), NN) for w, x in zip(wides, out)]
        out = [x + dot1(x, on_diagonal(e)) for x, e in zip(out, errs)]
    return out


NEWTON = 2


def invert(fac, inv_h, inv_l, slots):
    n = fac.shape[1]
    half, q = n // 2, n // 4
    wides = []
    for s in slots:
        for o in (0, half):
            wides.append(
                jnp.concatenate([fac[s, o : o + q, o : o + q], fac[s, o + q : o + half, o + q : o + half]], axis=1)
            )
    invs = pair_inverses(wides)
    parts = [(split(w[:, :q]), split(w[:, q:])) for w in invs]
    lows = [
        dot3(split(fac[s, o + q : o + half, o : o + q]), parts[2 * i + j][0], NN)
        for i, s in enumerate(slots)
        for j, o in enumerate((0, half))
    ]
    corners = [split(-dot3(p[1], split(m), NN)) for p, m in zip(parts, lows)]
    zero = jnp.zeros((q, q), BF16)
    for i, s in enumerate(slots):
        for j, o in enumerate((0, half)):
            (a, d), corner = parts[2 * i + j], corners[2 * i + j]
            for h, ref in enumerate((inv_h, inv_l)):
                ref[s, o : o + q, o : o + q] = a[h]
                ref[s, o : o + q, o + q : o + half] = zero
                ref[s, o + q : o + half, o : o + q] = corner[h]
                ref[s, o + q : o + half, o + q : o + half] = d[h]
    lows = [
        dot3(split(fac[s, half:, :half]), (inv_h[s, :half, :half], inv_l[s, :half, :half]), NN) for s in slots
    ]
    for s, low in zip(slots, lows):
        corner = -dot3((inv_h[s, half:, half:], inv_l[s, half:, half:]), split(low), NN)
        inv_h[s, half:, :half], inv_l[s, half:, :half] = split(corner)


class Net:
    def __init__(self, send_sems, recv_sems):
        self.sems = (send_sems, recv_sems)
        self.count = 0
        self.sent = []

    def send(self, source, target, device):
        copy = pltpu.make_async_remote_copy(
            src_ref=source,
            dst_ref=target,
            send_sem=self.sems[0].at[self.count],
            recv_sem=self.sems[1].at[self.count],
            device_id=device,
            device_id_type=pl.DeviceIdType.MESH,
        )
        copy.start()
        self.count += 1
        self.sent.append(copy)
        return copy

    def drain(self):
        for copy in self.sent:
            copy.wait_send()


FAR, NEXT, PREV, OWN = 0, 1, 2, 3
OFFSETS = (2, 1, 3, 0)


class Ring:
    def __init__(self, net, piece, up, down, far_in, out, near_in):
        self.net, self.piece, self.up, self.down = net, piece, up, down
        self.far_in, self.out, self.near_in = far_in, out, near_in

    def far(self):
        self.far_up = self.net.send(self.piece(FAR, 0), self.far_in.at[0], self.up)
        self.far_down = self.net.send(self.piece(FAR, 1), self.far_in.at[1], self.down)

    def near_up(self):
        self.n01 = self.net.send(self.piece(NEXT, 1), self.near_in.at[0, 1], self.up)

    def near_down(self):
        self.n10 = self.net.send(self.piece(PREV, 0), self.near_in.at[1, 0], self.down)

    def mid_up(self):
        self.far_up.wait_recv()
        self.out[0] = self.piece(NEXT, 0)[...] + self.far_in[0]
        self.n00 = self.net.send(self.out.at[0], self.near_in.at[0, 0], self.up)

    def mid_down(self):
        self.far_down.wait_recv()
        self.out[1] = self.piece(PREV, 1)[...] + self.far_in[1]
        self.n11 = self.net.send(self.out.at[1], self.near_in.at[1, 1], self.down)

    def end(self):
        for copy in (self.n01, self.n10, self.n00, self.n11):
            copy.wait_recv()
        return [self.piece(OWN, h)[...] + self.near_in[0, h] + self.near_in[1, h] for h in range(2)]


def fused_kernel(
    counts_hbm, blocks_hbm, fac_hbm, bf_hbm, bb_hbm, out_f, out_b, out_d,
    counts, blocks,
    fac, rhs, inv_h, inv_l, y0_h, y0_l, y1_h, y1_l, first, band, diag,
    core_in, held, z_far, z_out, z_near, z_sum, y_in, x_all, full,
    b_far, b_out, b_near, b_send, b_in, b_keep, d_in, d_far, d_out, d_near,
    load_sems, send_sems, recv_sems,
):
    b, s = lax.axis_index("branch"), lax.axis_index("scen")
    z, y_hi, core = b // 4, (b // 2) % 2, b % 2
    x, y_lo = s // 2, s % 2
    y = 2 * y_hi + y_lo
    cap, n, w = bf_hbm.shape
    half = w // 2
    halves = (pl.ds(0, half), pl.ds(half, half))
    net = Net(send_sems, recv_sems)

    fac_loads = [pltpu.make_async_copy(fac_hbm.at[t], fac.at[t], load_sems.at[t]) for t in range(cap)]
    rest = [(counts_hbm, counts), (blocks_hbm, blocks)]
    for t in range(cap):
        rest.append((bf_hbm.at[t], rhs.at[t, :, pl.ds(0, w)]))
        rest.append((bb_hbm.at[t], rhs.at[t, :, pl.ds(w, w)]))
    rest_loads = [pltpu.make_async_copy(a, c, load_sems.at[cap + i]) for i, (a, c) in enumerate(rest)]
    for copy in fac_loads + rest_loads:
        copy.start()

    other_core = (b + 1 - 2 * core, s)
    z_up, z_down = (((z + 1) % 4) * 4 + b % 4, s), (((z + 3) % 4) * 4 + b % 4, s)
    y_peers = []
    for d in (1, 2, 3):
        there = (y + d) % 4
        y_peers.append((z * 4 + (there // 2) * 2 + core, x * 2 + there % 2))
    x_peers = [(b, ((x + d) % 4) * 2 + y_lo) for d in (1, 2, 3)]
    x_up, x_down = x_peers[0], x_peers[2]
    y_near = (b, x * 2 + 1 - y_lo)
    barrier = pltpu.get_barrier_semaphore()
    greeted = [other_core, z_up, z_down] + y_peers + x_peers
    for peer in greeted:
        pl.semaphore_signal(barrier, inc=1, device_id=peer, device_id_type=pl.DeviceIdType.MESH)

    for copy in fac_loads:
        copy.wait()
    invert(fac, inv_h, inv_l, range(cap))
    for copy in rest_loads:
        copy.wait()

    first[...] = jnp.zeros_like(first)

    def chosen(t, shape):
        return jnp.broadcast_to(jnp.where(t < counts[0], blocks[t] % 2, 2), shape)

    def solve(t, start, y_h, y_l):
        top = (inv_h[t, :half, :half], inv_l[t, :half, :half])
        low = (inv_h[t, half:, :], inv_l[t, half:, :])
        live = chosen(t, (half, half)) < 2
        for cols in halves:
            right = split(rhs[t, :, pl.ds(start + cols.start, half)])
            up = dot3(top, (right[0][:half], right[1][:half]), NN)
            y_h[t, :half, cols], y_l[t, :half, cols] = split(jnp.where(live, up, 0.0))
            down = dot3(low, right, NN)
            y_h[t, half:, cols], y_l[t, half:, cols] = split(jnp.where(live, down, 0.0))

    @pl.loop(0, cap)
    def _(t):
        solve(t, 0, y0_h, y0_l)
        for i in range(0, w, half):
            left = (y0_h[t, :, pl.ds(i, half)], y0_l[t, :, pl.ds(i, half)])
            for j in range(0, i + half, half):
                right = (y0_h[t, :, pl.ds(j, half)], y0_l[t, :, pl.ds(j, half)])
                first[pl.ds(i, half), pl.ds(j, half)] += dot3(left, right, TN)

    first[:half, half:] = first[half:, :half].T

    pl.semaphore_wait(barrier, len(greeted))
    rows_core = pl.multiple_of(core * half, half)
    core_rows, core_far = pl.ds(rows_core, half), pl.ds(pl.multiple_of((1 - core) * half, half), half)
    core_copy = net.send(first.at[core_far], core_in, other_core)

    @pl.loop(0, cap)
    def _(t):
        solve(t, w, y1_h, y1_l)

    quarter = half // 2

    def place(role):
        return (x + OFFSETS[role]) % 4

    def band_terms(pair):
        cols = pl.ds(pl.multiple_of((place(pair[0]) % 2) * half, half), half)
        for role in pair:
            band[role] = jnp.zeros((half, w), F32)

        @pl.loop(0, cap)
        def _(t):
            which = chosen(t, (half, w))
            term = dot3((y1_h[t, :, cols], y1_l[t, :, cols]), (y0_h[t], y0_l[t]), TN)
            for role in pair:
                band[role] += jnp.where(which == place(role) // 2, term, 0.0)

    def diag_terms(pair):
        cols = [pl.ds(pl.multiple_of(place(role) * quarter, quarter), quarter) for role in pair]
        for role in pair:
            diag[role] = jnp.zeros((half, w), F32)

        @pl.loop(0, cap)
        def _(t):
            which = chosen(t, (quarter, w))
            left = [jnp.concatenate([y[t, :, c] for c in cols], axis=1) for y in (y1_h, y1_l)]
            term = dot3(left, (y1_h[t], y1_l[t]), TN)
            for i, role in enumerate(pair):
                for k in range(2):
                    part = jnp.where(which == k, term[i * quarter : (i + 1) * quarter], 0.0)
                    diag[role, pl.ds(k * quarter, quarter)] += part

    sub, drow = half // 2, quarter // 2
    bands = []
    for chunk, y_to in enumerate((1 - y_lo, y_lo)):

        def band_piece(role, h, y_to=y_to):
            return band.at[role, pl.ds(pl.multiple_of(y_to * sub, sub), sub), halves[h]]

        bands.append(Ring(net, band_piece, x_up, x_down, b_far.at[chunk], b_out.at[chunk], b_near.at[chunk]))

    def diag_rows(role, k, y_to):
        return diag.at[role, pl.ds(pl.multiple_of(k * quarter + y_to * drow, drow), drow), :]

    def diag_send(role):
        return [net.send(diag_rows(role, k, 1 - y_lo), d_in.at[role, k], y_near) for k in range(2)]

    def diag_take(copies, role):
        for k, copy in enumerate(copies):
            copy.wait_recv()
            d_in[role, k] += diag_rows(role, k, y_lo)[...]

    diags = Ring(net, lambda role, h: d_in.at[role, :, :, halves[h]], x_up, x_down, d_far, d_out, d_near)

    zrow = half // 4
    z_ring = Ring(
        net,
        lambda role, h: held.at[pl.ds(pl.multiple_of(((z + OFFSETS[role]) % 4) * zrow, zrow), zrow), halves[h]],
        z_up, z_down, z_far, z_out, z_near,
    )

    core_copy.wait_recv()
    held[...] = first[core_rows] + core_in[...]
    z_ring.far()
    z_ring.near_up()
    z_ring.near_down()
    diag_terms((FAR, OWN))
    d0 = diag_send(FAR)
    z_ring.mid_up()
    z_ring.mid_down()
    band_terms((FAR, OWN))
    bands[0].far()
    bands[1].far()
    diag_terms((NEXT, PREV))
    z_sum[:, :half], z_sum[:, half:] = z_ring.end()
    yrow = zrow // 4
    y_copies = []
    for d in (1, 2, 3):
        piece = z_sum.at[pl.ds(pl.multiple_of(((y + d) % 4) * yrow, yrow), yrow)]
        y_copies.append(net.send(piece, y_in.at[d - 1], y_peers[d - 1]))
    d1 = diag_send(NEXT)
    band_terms((NEXT, PREV))
    bands[0].near_up()
    bands[0].near_down()
    for copy in y_copies:
        copy.wait_recv()
    own = z_sum[pl.ds(pl.multiple_of(y * yrow, yrow), yrow)]
    x_all[x] = own + y_in[0] + y_in[1] + y_in[2]
    x_copies = [net.send(x_all.at[x], x_all.at[x], peer) for peer in x_peers]
    d2 = diag_send(PREV)
    bands[0].mid_up()
    bands[0].mid_down()
    diag_take(d0, FAR)
    diags.far()
    bands[1].near_up()
    bands[1].near_down()
    for copy in x_copies:
        copy.wait_recv()
    z_rows = rows_core + z * zrow
    y_rows = pl.ds(pl.multiple_of(z_rows + y * yrow, yrow), yrow)
    full[y_rows] = (x_all[0] + x_all[1]) + (x_all[2] + x_all[3])
    y_back = [net.send(full.at[y_rows], full.at[y_rows], peer) for peer in y_peers]
    d3 = diag_send(OWN)
    bands[1].mid_up()
    bands[1].mid_down()
    diag_take(d1, NEXT)
    diags.near_up()
    diags.mid_up()
    b_send[:, :half], b_send[:, half:] = bands[0].end()
    cross = net.send(b_send, b_in, y_near)
    diag_take(d2, PREV)
    diags.near_down()
    diags.mid_down()

    for copy in y_back:
        copy.wait_recv()

    def z_block(offset):
        return pl.ds(pl.multiple_of(rows_core + ((z + offset) % 4) * zrow, zrow), zrow)

    mine = full.at[z_block(0)]
    up_copy, down_copy = net.send(mine, mine, z_up), net.send(mine, mine, z_down)
    core_backs = [net.send(mine, mine, other_core)]
    b_keep[:, :half], b_keep[:, half:] = bands[1].end()
    up_copy.wait_recv()
    below = full.at[z_block(3)]
    pass_up = net.send(full.at[z_block(3), halves[0]], full.at[z_block(3), halves[0]], z_up)
    core_backs.append(net.send(below, below, other_core))
    down_copy.wait_recv()
    above = full.at[z_block(1)]
    pass_down = net.send(full.at[z_block(1), halves[1]], full.at[z_block(1), halves[1]], z_down)
    core_backs.append(net.send(above, above, other_core))
    diag_take(d3, OWN)
    pass_up.wait_recv()
    pass_down.wait_recv()
    far = full.at[z_block(2)]
    core_backs.append(net.send(far, far, other_core))
    for h, term in enumerate(diags.end()):
        out_d[:, :, halves[h]] = term
    cross.wait_recv()
    out_b[...] = b_keep[...] + b_in[...]
    for copy in core_backs:
        copy.wait_recv()
    out_f[...] = full[...]
    net.drain()


def fused(counts, blocks, factors, b_first, b_branch, c_first, c_band, c_diag):
    cap, n, w = b_first.shape
    half = w // 2
    k, drow = c_diag.shape[0], c_diag.shape[1]
    sub = c_band.shape[0]
    zrow = half // 4
    yrow = zrow // 4
    vmem = pl.BlockSpec(memory_space=pltpu.VMEM)
    hbm = pl.BlockSpec(memory_space=HBM)
    v = lambda *shape: pltpu.VMEM(shape, F32)
    vb = lambda *shape: pltpu.VMEM(shape, BF16)
    return pl.pallas_call(
        fused_kernel,
        out_shape=tuple(jax.ShapeDtypeStruct(a.shape, F32) for a in (c_first, c_band, c_diag)),
        in_specs=[hbm] * 5,
        out_specs=(vmem, vmem, vmem),
        scratch_shapes=[
            pltpu.SMEM((1,), jnp.int32), pltpu.SMEM((cap,), jnp.int32),
            v(cap, n, n), v(cap, n, 2 * w), vb(cap, n, n), vb(cap, n, n),
            vb(cap, n, w), vb(cap, n, w), vb(cap, n, w), vb(cap, n, w),
            v(w, w), v(4, half, w), v(4, half, w),
            v(half, w), v(half, w), v(2, zrow, half), v(2, zrow, half), v(2, 2, zrow, half), v(zrow, w),
            v(3, yrow, w), v(4, yrow, w), v(w, w),
            v(2, 2, sub, half), v(2, 2, sub, half), v(2, 2, 2, sub, half), v(sub, w), v(sub, w), v(sub, w),
            v(4, k, drow, w), v(2, k, drow, half), v(2, k, drow, half), v(2, 2, k, drow, half),
            pltpu.SemaphoreType.DMA((3 * cap + 2,)),
            pltpu.SemaphoreType.DMA((64,)), pltpu.SemaphoreType.DMA((64,)),
        ],
        compiler_params=pltpu.CompilerParams(vmem_limit_bytes=50 << 20, collective_id=0, has_side_effects=True),
        name="schur",
    )(counts, blocks, factors, b_first, b_branch)


def finish_kernel(first, band, diag, cf, cb, cd, out_f, out_b, out_d, tf, tb, td, sems):
    copies = []
    half = first.shape[0] // 2
    for i in range(2):
        rows = pl.ds(i * half, half)
        tf[rows] = cf[rows] - first[rows]
        copies.append(pltpu.make_async_copy(tf.at[rows], out_f.at[rows], sems.at[i]))
        copies[-1].start()
    tb[...] = cb[...] - band[...]
    copies.append(pltpu.make_async_copy(tb, out_b, sems.at[2]))
    copies[-1].start()
    td[...] = cd[...] - diag[...]
    copies.append(pltpu.make_async_copy(td, out_d, sems.at[3]))
    copies[-1].start()
    for copy in copies:
        copy.wait()


def finish(first, band, diag, c_first, c_band, c_diag):
    vmem = pl.BlockSpec(memory_space=pltpu.VMEM)
    cs = (c_first, c_band, c_diag)
    return pl.pallas_call(
        finish_kernel,
        out_shape=tuple(jax.ShapeDtypeStruct(c.shape, F32) for c in cs),
        in_specs=[vmem] * 6,
        out_specs=(pl.BlockSpec(memory_space=HBM),) * 3,
        scratch_shapes=[pltpu.VMEM(c.shape, F32) for c in cs] + [pltpu.SemaphoreType.DMA((4,))],
        compiler_params=pltpu.CompilerParams(vmem_limit_bytes=8 << 20),
        name="finish",
    )(first, band, diag, *cs)


HBM = pltpu.HBM


def shards(counts, blocks, factors, b_first, b_branch, c_first, c_band, c_diag):
    first, band, diag = fused(counts, blocks, factors, b_first, b_branch, c_first, c_band, c_diag)
    return finish(first, band, diag, c_first, c_band, c_diag)


def solution(mesh):
    placed = (
        P(("branch", "scen")),
        P(("branch", "scen")),
        P(("branch", "scen"), None, None),
        P(("branch", "scen"), None, None),
        P(("branch", "scen"), None, None),
        P(),
        P(("branch", "scen"), None),
        P("branch", "scen", None),
    )
    return jax.shard_map(
        shards,
        mesh=mesh,
        in_specs=placed,
        out_specs=(P(), P(("branch", "scen"), None), P("branch", "scen", None)),
        check_vma=False,
    )
```

```python
import jax
import jax.numpy as jnp
from jax import lax
from jax.experimental import pallas as pl
from jax.experimental.pallas import tpu as pltpu
from jax.sharding import PartitionSpec as P

F32, BF16 = jnp.float32, jnp.bfloat16


def split(value):
    high = value.astype(BF16)
    return high, (value - high.astype(F32)).astype(BF16)


def dot3(left, right, dims):
    (lh, ll), (rh, rl) = left, right
    one = lambda a, b: lax.dot_general(a, b, (dims, ((), ())), preferred_element_type=F32)
    return one(lh, rl) + one(ll, rh) + one(lh, rh)


NN = ((1,), (0,))
TN = ((0,), (0,))


def on_diagonal(wide):
    lane = lax.broadcasted_iota(jnp.int32, wide.shape, 1)
    left = lane < wide.shape[0]
    zero = jnp.zeros_like(wide)
    return jnp.concatenate([jnp.where(left, wide, zero), jnp.where(left, zero, wide)], axis=0)


def dot1(left, right):
    return lax.dot_general(left.astype(BF16), right.astype(BF16), (NN, ((), ())), preferred_element_type=F32)


def pair_inverses(wides):
    rows, cols = wides[0].shape
    r = lax.broadcasted_iota(jnp.int32, (rows, cols), 0)
    c = lax.broadcasted_iota(jnp.int32, (rows, cols), 1) & (rows - 1)
    eye = r == c
    out = []
    for wide in wides:
        pivots = jnp.where(eye, wide, 0.0)
        by_col = 1.0 / jnp.sum(pivots, axis=0, keepdims=True)
        by_row = 1.0 / jnp.concatenate(
            [
                jnp.broadcast_to(jnp.sum(pivots[:, i : i + rows], axis=1, keepdims=True), (rows, rows))
                for i in range(0, cols, rows)
            ],
            axis=1,
        )
        pairs = ((r >> 1) == (c >> 1)) & (r > c)
        out.append(jnp.where(eye, by_row, 0.0) - jnp.where(pairs, wide * by_col * by_row, 0.0))
    shift = 1
    while (1 << shift) < rows:
        below = ((r >> (shift + 1)) == (c >> (shift + 1))) & ((r >> shift) > (c >> shift))
        mids = [dot1(jnp.where(below, w, 0.0), on_diagonal(x)) for w, x in zip(wides, out)]
        out = [x - dot1(x, on_diagonal(m)) for x, m in zip(out, mids)]
        shift += 1
    unit = jnp.where(eye, 1.0, 0.0)
    for _ in range(NEWTON):
        errs = [unit - dot3(split(w), split(on_diagonal(x)), NN) for w, x in zip(wides, out)]
        out = [x + dot1(x, on_diagonal(e)) for x, e in zip(out, errs)]
    return out


NEWTON = 2


def invert(fac, inv_h, inv_l, slots):
    n = fac.shape[1]
    half, q = n // 2, n // 4
    wides = []
    for s in slots:
        for o in (0, half):
            wides.append(
                jnp.concatenate([fac[s, o : o + q, o : o + q], fac[s, o + q : o + half, o + q : o + half]], axis=1)
            )
    invs = pair_inverses(wides)
    parts = [(split(w[:, :q]), split(w[:, q:])) for w in invs]
    lows = [
        dot3(split(fac[s, o + q : o + half, o : o + q]), parts[2 * i + j][0], NN)
        for i, s in enumerate(slots)
        for j, o in enumerate((0, half))
    ]
    corners = [split(-dot3(p[1], split(m), NN)) for p, m in zip(parts, lows)]
    zero = jnp.zeros((q, q), BF16)
    for i, s in enumerate(slots):
        for j, o in enumerate((0, half)):
            (a, d), corner = parts[2 * i + j], corners[2 * i + j]
            for h, ref in enumerate((inv_h, inv_l)):
                ref[s, o : o + q, o : o + q] = a[h]
                ref[s, o : o + q, o + q : o + half] = zero
                ref[s, o + q : o + half, o : o + q] = corner[h]
                ref[s, o + q : o + half, o + q : o + half] = d[h]
    lows = [
        dot3(split(fac[s, half:, :half]), (inv_h[s, :half, :half], inv_l[s, :half, :half]), NN) for s in slots
    ]
    for s, low in zip(slots, lows):
        corner = -dot3((inv_h[s, half:, half:], inv_l[s, half:, half:]), split(low), NN)
        inv_h[s, half:, :half], inv_l[s, half:, :half] = split(corner)


class Net:
    def __init__(self, send_sems, recv_sems):
        self.sems = (send_sems, recv_sems)
        self.count = 0
        self.sent = []

    def send(self, source, target, device):
        copy = pltpu.make_async_remote_copy(
            src_ref=source,
            dst_ref=target,
            send_sem=self.sems[0].at[self.count],
            recv_sem=self.sems[1].at[self.count],
            device_id=device,
            device_id_type=pl.DeviceIdType.MESH,
        )
        copy.start()
        self.count += 1
        self.sent.append(copy)
        return copy

    def drain(self):
        for copy in self.sent:
            copy.wait_send()


FAR, NEXT, PREV, OWN = 0, 1, 2, 3
OFFSETS = (2, 1, 3, 0)


class Ring:
    def __init__(self, net, piece, up, down, far_in, out, near_in):
        self.net, self.piece, self.up, self.down = net, piece, up, down
        self.far_in, self.out, self.near_in = far_in, out, near_in

    def far(self):
        self.far_up = self.net.send(self.piece(FAR, 0), self.far_in.at[0], self.up)
        self.far_down = self.net.send(self.piece(FAR, 1), self.far_in.at[1], self.down)

    def near_up(self):
        self.n01 = self.net.send(self.piece(NEXT, 1), self.near_in.at[0, 1], self.up)

    def near_down(self):
        self.n10 = self.net.send(self.piece(PREV, 0), self.near_in.at[1, 0], self.down)

    def mid_up(self):
        self.far_up.wait_recv()
        self.out[0] = self.piece(NEXT, 0)[...] + self.far_in[0]
        self.n00 = self.net.send(self.out.at[0], self.near_in.at[0, 0], self.up)

    def mid_down(self):
        self.far_down.wait_recv()
        self.out[1] = self.piece(PREV, 1)[...] + self.far_in[1]
        self.n11 = self.net.send(self.out.at[1], self.near_in.at[1, 1], self.down)

    def end(self):
        for copy in (self.n01, self.n10, self.n00, self.n11):
            copy.wait_recv()
        return [self.piece(OWN, h)[...] + self.near_in[0, h] + self.near_in[1, h] for h in range(2)]


def fused_kernel(
    counts_hbm, blocks_hbm, fac_hbm, bf_hbm, bb_hbm, out_f, out_b, out_d,
    counts, blocks,
    fac, rhs, inv_h, inv_l, y0_h, y0_l, y1_h, y1_l, first, band, diag,
    core_in, held, z_far, z_out, z_near, z_sum, y_in, x_all, full,
    b_far, b_out, b_near, b_send, b_in, b_keep, d_in, d_far, d_out, d_near,
    load_sems, send_sems, recv_sems,
):
    b, s = lax.axis_index("branch"), lax.axis_index("scen")
    z, y_hi, core = b // 4, (b // 2) % 2, b % 2
    x, y_lo = s // 2, s % 2
    y = 2 * y_hi + y_lo
    cap, n, w = bf_hbm.shape
    half = w // 2
    halves = (pl.ds(0, half), pl.ds(half, half))
    net = Net(send_sems, recv_sems)

    fac_loads = [pltpu.make_async_copy(fac_hbm.at[t], fac.at[t], load_sems.at[t]) for t in range(cap)]
    rest = [(counts_hbm, counts), (blocks_hbm, blocks)]
    for t in range(cap):
        rest.append((bf_hbm.at[t], rhs.at[t, :, pl.ds(0, w)]))
        rest.append((bb_hbm.at[t], rhs.at[t, :, pl.ds(w, w)]))
    rest_loads = [pltpu.make_async_copy(a, c, load_sems.at[cap + i]) for i, (a, c) in enumerate(rest)]
    for copy in fac_loads + rest_loads:
        copy.start()

    other_core = (b + 1 - 2 * core, s)
    z_up, z_down = (((z + 1) % 4) * 4 + b % 4, s), (((z + 3) % 4) * 4 + b % 4, s)
    y_peers = []
    for d in (1, 2, 3):
        there = (y + d) % 4
        y_peers.append((z * 4 + (there // 2) * 2 + core, x * 2 + there % 2))
    x_peers = [(b, ((x + d) % 4) * 2 + y_lo) for d in (1, 2, 3)]
    x_up, x_down = x_peers[0], x_peers[2]
    y_near = (b, x * 2 + 1 - y_lo)
    barrier = pltpu.get_barrier_semaphore()
    greeted = [other_core, z_up, z_down] + y_peers + x_peers
    for peer in greeted:
        pl.semaphore_signal(barrier, inc=1, device_id=peer, device_id_type=pl.DeviceIdType.MESH)

    for copy in fac_loads:
        copy.wait()
    invert(fac, inv_h, inv_l, range(cap))
    for copy in rest_loads:
        copy.wait()

    zrow = half // 4
    z_ring = Ring(
        net,
        lambda role, h: held.at[pl.ds(pl.multiple_of(((z + OFFSETS[role]) % 4) * zrow, zrow), zrow), halves[h]],
        z_up, z_down, z_far, z_out, z_near,
    )

    first[...] = jnp.zeros_like(first)

    def chosen(t, shape):
        return jnp.broadcast_to(jnp.where(t < counts[0], blocks[t] % 2, 2), shape)

    def solve(t, start, y_h, y_l):
        top = (inv_h[t, :half, :half], inv_l[t, :half, :half])
        low = (inv_h[t, half:, :], inv_l[t, half:, :])
        live = chosen(t, (half, half)) < 2
        for cols in halves:
            right = split(rhs[t, :, pl.ds(start + cols.start, half)])
            up = dot3(top, (right[0][:half], right[1][:half]), NN)
            y_h[t, :half, cols], y_l[t, :half, cols] = split(jnp.where(live, up, 0.0))
            down = dot3(low, right, NN)
            y_h[t, half:, cols], y_l[t, half:, cols] = split(jnp.where(live, down, 0.0))

    @pl.loop(0, cap, unroll=True)
    def _(t):
        solve(t, 0, y0_h, y0_l)
        for i in range(0, w, half):
            left = (y0_h[t, :, pl.ds(i, half)], y0_l[t, :, pl.ds(i, half)])
            for j in range(0, i + half, half):
                right = (y0_h[t, :, pl.ds(j, half)], y0_l[t, :, pl.ds(j, half)])
                first[pl.ds(i, half), pl.ds(j, half)] += dot3(left, right, TN)

    first[:half, half:] = first[half:, :half].T

    pl.semaphore_wait(barrier, len(greeted))
    rows_core = pl.multiple_of(core * half, half)
    core_rows, core_far = pl.ds(rows_core, half), pl.ds(pl.multiple_of((1 - core) * half, half), half)
    core_copy = net.send(first.at[core_far], core_in, other_core)

    @pl.loop(0, cap - 1, unroll=True)
    def _(t):
        solve(t, w, y1_h, y1_l)

    core_copy.wait_recv()
    held[...] = first[core_rows] + core_in[...]
    z_ring.far()
    z_ring.near_up()
    z_ring.near_down()
    solve(cap - 1, w, y1_h, y1_l)

    quarter = half // 2

    def place(role):
        return (x + OFFSETS[role]) % 4

    def band_terms(pair):
        cols = pl.ds(pl.multiple_of((place(pair[0]) % 2) * half, half), half)
        for role in pair:
            band[role] = jnp.zeros((half, w), F32)

        @pl.loop(0, cap, unroll=True)
        def _(t):
            which = chosen(t, (half, w))
            term = dot3((y1_h[t, :, cols], y1_l[t, :, cols]), (y0_h[t], y0_l[t]), TN)
            for role in pair:
                band[role] += jnp.where(which == place(role) // 2, term, 0.0)

    def diag_terms(pair):
        cols = [pl.ds(pl.multiple_of(place(role) * quarter, quarter), quarter) for role in pair]
        for role in pair:
            diag[role] = jnp.zeros((half, w), F32)

        @pl.loop(0, cap, unroll=True)
        def _(t):
            which = chosen(t, (quarter, w))
            left = [jnp.concatenate([y[t, :, c] for c in cols], axis=1) for y in (y1_h, y1_l)]
            term = dot3(left, (y1_h[t], y1_l[t]), TN)
            for i, role in enumerate(pair):
                for k in range(2):
                    part = jnp.where(which == k, term[i * quarter : (i + 1) * quarter], 0.0)
                    diag[role, pl.ds(k * quarter, quarter)] += part

    sub, drow = half // 2, quarter // 2
    bands = []
    for chunk, y_to in enumerate((1 - y_lo, y_lo)):

        def band_piece(role, h, y_to=y_to):
            return band.at[role, pl.ds(pl.multiple_of(y_to * sub, sub), sub), halves[h]]

        bands.append(Ring(net, band_piece, x_up, x_down, b_far.at[chunk], b_out.at[chunk], b_near.at[chunk]))

    def diag_rows(role, k, y_to):
        return diag.at[role, pl.ds(pl.multiple_of(k * quarter + y_to * drow, drow), drow), :]

    def diag_send(role):
        return [net.send(diag_rows(role, k, 1 - y_lo), d_in.at[role, k], y_near) for k in range(2)]

    def diag_take(copies, role):
        for k, copy in enumerate(copies):
            copy.wait_recv()
            d_in[role, k] += diag_rows(role, k, y_lo)[...]

    diags = Ring(net, lambda role, h: d_in.at[role, :, :, halves[h]], x_up, x_down, d_far, d_out, d_near)

    diag_terms((FAR, OWN))
    d0 = diag_send(FAR)
    z_ring.mid_up()
    z_ring.mid_down()
    band_terms((FAR, OWN))
    bands[0].far()
    bands[1].far()
    z_sum[:, :half], z_sum[:, half:] = z_ring.end()
    yrow = zrow // 4
    y_copies = []
    for d in (1, 2, 3):
        piece = z_sum.at[pl.ds(pl.multiple_of(((y + d) % 4) * yrow, yrow), yrow)]
        y_copies.append(net.send(piece, y_in.at[d - 1], y_peers[d - 1]))
    diag_terms((NEXT, PREV))
    d1 = diag_send(NEXT)
    band_terms((NEXT, PREV))
    for copy in y_copies:
        copy.wait_recv()
    own = z_sum[pl.ds(pl.multiple_of(y * yrow, yrow), yrow)]
    x_all[x] = own + y_in[0] + y_in[1] + y_in[2]
    x_copies = [net.send(x_all.at[x], x_all.at[x], peer) for peer in x_peers]
    bands[0].near_up()
    bands[0].near_down()
    bands[0].mid_up()
    bands[0].mid_down()
    diag_take(d0, FAR)
    diags.far()
    for copy in x_copies:
        copy.wait_recv()
    z_rows = rows_core + z * zrow
    y_rows = pl.ds(pl.multiple_of(z_rows + y * yrow, yrow), yrow)
    full[y_rows] = (x_all[0] + x_all[1]) + (x_all[2] + x_all[3])
    y_back = [net.send(full.at[y_rows], full.at[y_rows], peer) for peer in y_peers]
    d2 = diag_send(PREV)
    d3 = diag_send(OWN)
    bands[1].near_up()
    bands[1].near_down()
    bands[1].mid_up()
    bands[1].mid_down()
    diag_take(d1, NEXT)
    diags.near_up()
    diags.mid_up()
    for copy in y_back:
        copy.wait_recv()

    def z_block(offset):
        return pl.ds(pl.multiple_of(rows_core + ((z + offset) % 4) * zrow, zrow), zrow)

    mine = full.at[z_block(0)]
    up_copy, down_copy = net.send(mine, mine, z_up), net.send(mine, mine, z_down)
    core_backs = [net.send(mine, mine, other_core)]
    b_send[:, :half], b_send[:, half:] = bands[0].end()
    cross = net.send(b_send, b_in, y_near)
    up_copy.wait_recv()
    below = full.at[z_block(3)]
    pass_up = net.send(full.at[z_block(3), halves[0]], full.at[z_block(3), halves[0]], z_up)
    core_backs.append(net.send(below, below, other_core))
    down_copy.wait_recv()
    above = full.at[z_block(1)]
    pass_down = net.send(full.at[z_block(1), halves[1]], full.at[z_block(1), halves[1]], z_down)
    core_backs.append(net.send(above, above, other_core))
    diag_take(d2, PREV)
    diags.near_down()
    diags.mid_down()
    b_keep[:, :half], b_keep[:, half:] = bands[1].end()
    pass_up.wait_recv()
    pass_down.wait_recv()
    far = full.at[z_block(2)]
    core_backs.append(net.send(far, far, other_core))
    diag_take(d3, OWN)
    for copy in core_backs:
        copy.wait_recv()
    out_f[...] = full[...]
    for h, term in enumerate(diags.end()):
        out_d[:, :, halves[h]] = term
    cross.wait_recv()
    out_b[...] = b_keep[...] + b_in[...]
    net.drain()


def fused(counts, blocks, factors, b_first, b_branch, c_first, c_band, c_diag):
    cap, n, w = b_first.shape
    half = w // 2
    k, drow = c_diag.shape[0], c_diag.shape[1]
    sub = c_band.shape[0]
    zrow = half // 4
    yrow = zrow // 4
    vmem = pl.BlockSpec(memory_space=pltpu.VMEM)
    hbm = pl.BlockSpec(memory_space=HBM)
    v = lambda *shape: pltpu.VMEM(shape, F32)
    vb = lambda *shape: pltpu.VMEM(shape, BF16)
    return pl.pallas_call(
        fused_kernel,
        out_shape=tuple(jax.ShapeDtypeStruct(a.shape, F32) for a in (c_first, c_band, c_diag)),
        in_specs=[hbm] * 5,
        out_specs=(vmem, vmem, vmem),
        scratch_shapes=[
            pltpu.SMEM((1,), jnp.int32), pltpu.SMEM((cap,), jnp.int32),
            v(cap, n, n), v(cap, n, 2 * w), vb(cap, n, n), vb(cap, n, n),
            vb(cap, n, w), vb(cap, n, w), vb(cap, n, w), vb(cap, n, w),
            v(w, w), v(4, half, w), v(4, half, w),
            v(half, w), v(half, w), v(2, zrow, half), v(2, zrow, half), v(2, 2, zrow, half), v(zrow, w),
            v(3, yrow, w), v(4, yrow, w), v(w, w),
            v(2, 2, sub, half), v(2, 2, sub, half), v(2, 2, 2, sub, half), v(sub, w), v(sub, w), v(sub, w),
            v(4, k, drow, w), v(2, k, drow, half), v(2, k, drow, half), v(2, 2, k, drow, half),
            pltpu.SemaphoreType.DMA((3 * cap + 2,)),
            pltpu.SemaphoreType.DMA((64,)), pltpu.SemaphoreType.DMA((64,)),
        ],
        compiler_params=pltpu.CompilerParams(vmem_limit_bytes=50 << 20, collective_id=0, has_side_effects=True),
        name="schur",
    )(counts, blocks, factors, b_first, b_branch)


def finish_kernel(first, band, diag, cf, cb, cd, out_f, out_b, out_d, tf, tb, td, sems):
    copies = []
    half = first.shape[0] // 2
    for i in range(2):
        rows = pl.ds(i * half, half)
        tf[rows] = cf[rows] - first[rows]
        copies.append(pltpu.make_async_copy(tf.at[rows], out_f.at[rows], sems.at[i]))
        copies[-1].start()
    tb[...] = cb[...] - band[...]
    copies.append(pltpu.make_async_copy(tb, out_b, sems.at[2]))
    copies[-1].start()
    td[...] = cd[...] - diag[...]
    copies.append(pltpu.make_async_copy(td, out_d, sems.at[3]))
    copies[-1].start()
    for copy in copies:
        copy.wait()


def finish(first, band, diag, c_first, c_band, c_diag):
    vmem = pl.BlockSpec(memory_space=pltpu.VMEM)
    cs = (c_first, c_band, c_diag)
    return pl.pallas_call(
        finish_kernel,
        out_shape=tuple(jax.ShapeDtypeStruct(c.shape, F32) for c in cs),
        in_specs=[vmem] * 6,
        out_specs=(pl.BlockSpec(memory_space=HBM),) * 3,
        scratch_shapes=[pltpu.VMEM(c.shape, F32) for c in cs] + [pltpu.SemaphoreType.DMA((4,))],
        compiler_params=pltpu.CompilerParams(vmem_limit_bytes=8 << 20),
        name="finish",
    )(first, band, diag, *cs)


HBM = pltpu.HBM


def shards(counts, blocks, factors, b_first, b_branch, c_first, c_band, c_diag):
    first, band, diag = fused(counts, blocks, factors, b_first, b_branch, c_first, c_band, c_diag)
    return finish(first, band, diag, c_first, c_band, c_diag)


def solution(mesh):
    placed = (
        P(("branch", "scen")),
        P(("branch", "scen")),
        P(("branch", "scen"), None, None),
        P(("branch", "scen"), None, None),
        P(("branch", "scen"), None, None),
        P(),
        P(("branch", "scen"), None),
        P("branch", "scen", None),
    )
    return jax.shard_map(
        shards,
        mesh=mesh,
        in_specs=placed,
        out_specs=(P(), P(("branch", "scen"), None), P("branch", "scen", None)),
        check_vma=False,
    )
```
